256 devices in a mesh: seq: 16 (over z, core), head: 16 (over x, y).
Axes of the slice: x: 4, y: 4, z: 8, core: 2. Of those that a mesh axis runs over, the one named last changes fastest.
Arguments:
- x_in: bfloat16 [16384, 8192], P('seq', 'head'), may hold values from -6 to 6
- z_gate: bfloat16 [16384, 8192], P('seq', 'head'), may hold values from -6 to 6
- b_in: bfloat16 [16384, 128], P('seq'), may hold values from -6.5 to 6.5
- c_in: bfloat16 [16384, 128], P('seq'), may hold values from -6 to 6
- dt_raw: float32 [16384, 128], P('seq', 'head'), may hold values from -7.5 to 263.144
- a_log: float32 [128], P('head'), may hold values from -12 to 3.5, as said below
- d_skip: float32 [128], P('head'), may hold values from 0.5 to 1.5
- conv_x: float32 [4, 8192], P(None, 'head'), may hold values from -3 to 3
- conv_bc: float32 [4, 256], replicated, may hold values from -0.8 to 0.8
- norm_gain: float32 [8192], P('head'), may hold values from 0.1 to 1.9
- w_out: bfloat16 [8192, 4096], P('head'), may hold values from -0.0625 to 0.0625
Outputs:
- mixed: bfloat16 [16384, 4096], P(('seq', 'head'))
The draws below stay inside these ranges and needn't reach their ends.
Inputs may be any that keep to these rules, and one draw needn't show every extreme that they name: `a_log`: logarithm of each head's decay rate.
All inputs are finite; a program needn't handle non-finite values.
Results may differ from the reference program's by a relative error of at most 0.018.
Values may be sent and summed in bfloat16 or wider, within the bound.
No kernel may reach another device: no remote copies, remote signals or barrier semaphores. Data moves between devices by JAX's collectives and lax.ppermute only.
A program may use at most 64 MiB of HBM per device.

```python
import jax
import jax.numpy as jnp
from jax import lax

D = 4096
HEADS = 128
HEAD_DIM = 64
STATE = 128
KCONV = 4
SPAN = 256
SEQ_SPAN_LOCAL = 1024
INNER = 8192
FRAME_LENGTH = 16384
N_HEAD = 16


def head_offsets(key):
    return jax.random.uniform(jax.random.fold_in(key, 41), (HEADS,), jnp.float32, -1.2, 1.2)


def head_step_mean(key):
    return jax.nn.softplus(-4.75 + head_offsets(key))


def pulse_plan(key):
    live_key, line_key, depth_key = jax.random.split(jax.random.fold_in(key, 57), 3)
    cluster_total = FRAME_LENGTH // SEQ_SPAN_LOCAL
    pulse_live = jax.random.uniform(live_key, (cluster_total,), jnp.float32) < 0.5
    pulse_line = jnp.floor(jax.random.uniform(line_key, (cluster_total,), jnp.float32, 0.0, 0.999) * SEQ_SPAN_LOCAL)
    depth = jax.random.uniform(depth_key, (cluster_total,), jnp.float32, 0.2, 0.5)
    rows = jnp.arange(FRAME_LENGTH)
    cluster_table = rows // SEQ_SPAN_LOCAL
    inside_segment = (rows % SEQ_SPAN_LOCAL).astype(jnp.float32)
    flagged = pulse_live[cluster_table] & (inside_segment == pulse_line[cluster_table])
    return (flagged, depth[cluster_table])


def bc_taps(key):
    sign_key, size_key = jax.random.split(jax.random.fold_in(key, 31), 2)
    signs = jnp.where(jax.random.uniform(sign_key, (2 * STATE,), jnp.float32) < 0.5, -1.0, 1.0)
    sizes = jax.random.uniform(size_key, (KCONV, 2 * STATE), jnp.float32, 0.1, 0.8)
    return sizes * signs[None, :]


def draw_conv_bc(key, part):
    return bc_taps(key).astype(jnp.float32)


def draw_b_in(key, part):
    taps = bc_taps(key)[:, :STATE]
    offset = -0.5 * jnp.sqrt(jnp.sum(taps * taps, axis=0)) / jnp.sum(taps, axis=0)
    noise = jnp.clip(jax.random.normal(jax.random.fold_in(key, 67), (FRAME_LENGTH, STATE), jnp.float32), -6.0, 6.0)
    flagged, _ = pulse_plan(key)
    nearby = flagged
    for lead in range(1, KCONV):
        nearby = nearby | jnp.concatenate([flagged[lead:], jnp.zeros((lead,), bool)])
    values = jnp.where(nearby[:, None], 0.003 * noise, noise + offset[None, :])
    return values.astype(jnp.bfloat16)


def draw_a_log(key, part):
    first, second, third = jax.random.split(jax.random.fold_in(key, 11), 3)
    step_mean = head_step_mean(key)
    share = 0.5
    slow = jax.random.uniform(first, (HEADS,), jnp.float32) < share
    keep = jax.random.uniform(second, (HEADS,), jnp.float32, 0.5, 2.0)
    slow_rate = keep / (step_mean * FRAME_LENGTH)
    reach = jax.random.uniform(third, (HEADS,), jnp.float32, 30.0, 50.0)
    fast_rate = 2.3 / (reach * step_mean)
    return jnp.log(jnp.where(slow, slow_rate, fast_rate)).astype(jnp.float32)


def draw_dt_raw(key, part):
    first, second = jax.random.split(jax.random.fold_in(key, 23), 2)
    cluster_total = FRAME_LENGTH // SEQ_SPAN_LOCAL
    noise = jnp.clip(0.4 * jax.random.normal(first, (FRAME_LENGTH, HEADS), jnp.float32), -0.75, 0.75)
    base = -4.75 + head_offsets(key)[None, :] + noise
    level = jax.random.uniform(second, (cluster_total,), jnp.float32, -0.8, 0.8)
    rows = jnp.arange(FRAME_LENGTH)
    cluster_table = rows // SEQ_SPAN_LOCAL
    flagged, depth_rows = pulse_plan(key)
    step_mean = head_step_mean(key)
    pulse_step = -jnp.log(1.0 - depth_rows)[:, None] * step_mean[None, :] * FRAME_LENGTH / 1.25
    pulse_raw = pulse_step + jnp.log(-jnp.expm1(-pulse_step))
    element_item = base + level[cluster_table][:, None]
    element_item = jnp.where(flagged[:, None], pulse_raw, element_item)
    return element_item.astype(jnp.float32)


def block_scale(stream_key, shape, cuts, smallest, largest):
    def one(dim, parts):
        heights = jax.random.uniform(jax.random.fold_in(jax.random.fold_in(stream_key, 6), dim), (parts,), jnp.float32, smallest / len(cuts), largest / len(cuts))
        return jnp.repeat(jnp.exp(heights), shape[dim] // parts).reshape((-1,) + (1,) * (len(shape) - dim - 1))

    gain = one(*cuts[0])
    for cut in cuts[1:]:
        gain = gain * one(*cut)
    return gain


def scatter_about(key, dims, deviation, most, cuts=(), held_as=jnp.bfloat16):
    factor_of = block_scale(key, dims, cuts, -0.22, 0.18) if cuts else 1.0
    values = jax.random.normal(key, dims, jnp.float32) * deviation * factor_of
    return jnp.minimum(jnp.maximum(values, -most), most).astype(held_as)


def setup_inputs(seed: int = 0) -> dict:
    key_list = jax.random.split(jax.random.key(seed), 12)
    x_in = scatter_about(key_list[0], (FRAME_LENGTH, INNER), 1.0, 6.0, ((0, 16), (1, 16)))
    z_gate = scatter_about(key_list[1], (FRAME_LENGTH, INNER), 1.0, 6.0, ((0, 16), (1, 16)))
    b_in = draw_b_in(jax.random.fold_in(key_list[11], 71), 0)
    c_in = scatter_about(key_list[3], (FRAME_LENGTH, STATE), 1.0, 6.0, ((0, 16),))
    dt_raw = draw_dt_raw(jax.random.fold_in(key_list[11], 71), 0)
    a_log = draw_a_log(jax.random.fold_in(key_list[11], 71), 0)
    d_skip = jnp.clip(0.5 + 1.0 * jax.random.uniform(key_list[6], (HEADS,), jnp.float32) ** block_scale(key_list[6], (HEADS,), ((0, 16),), -0.2, 0.2), 0.5, 1.5)
    conv_x = scatter_about(key_list[7], (KCONV, INNER), KCONV ** -0.5, 3.0, ((1, 16),), jnp.float32)
    conv_bc = draw_conv_bc(jax.random.fold_in(key_list[11], 71), 0)
    norm_gain = jnp.clip(1.0 + 0.18 * jax.random.normal(key_list[9], (INNER,), jnp.float32), 0.1, 1.9)
    w_out = scatter_about(key_list[10], (INNER, D), INNER ** -0.5, 0.0625, ((0, 16),))
    return {"x_in": x_in, "z_gate": z_gate, "b_in": b_in, "c_in": c_in, "dt_raw": dt_raw, "a_log": a_log, "d_skip": d_skip, "conv_x": conv_x, "conv_bc": conv_bc, "norm_gain": norm_gain, "w_out": w_out}


def causal_conv(values, rim, weight):
    n_rows = values.shape[0]
    padded = jnp.concatenate([rim.astype(jnp.float32), values.astype(jnp.float32)], axis=0)
    result = weight[0][None, :] * padded[0:n_rows]
    for offset in range(1, weight.shape[0]):
        result = result + weight[offset][None, :] * padded[offset:offset + n_rows]
    return jax.nn.silu(result).astype(jnp.bfloat16)

def span_step(memory, pieces):
    x_part, b_part, c_part, step_part, decay_part = pieces
    running = jnp.cumsum(decay_part, axis=0)
    length = x_part.shape[0]
    positions = lax.iota(jnp.int32, length)
    causal = positions[:, None] >= positions[None, :]
    spread = jnp.where(causal[:, :, None], running[:, None, :] - running[None, :, :], -1e+30)
    scores = jnp.dot(c_part, b_part.T, preferred_element_type=jnp.float32)
    b_wide = b_part.astype(jnp.float32)
    c_wide = c_part.astype(jnp.float32)
    mixing = jnp.exp(spread) * scores[:, :, None] * step_part[None, :, :]
    inside = jnp.einsum('ijh,jhp->ihp', mixing, x_part, precision=lax.Precision.HIGHEST)
    earlier = jnp.einsum('in,hpn->ihp', c_wide, memory, precision=lax.Precision.HIGHEST) * jnp.exp(running)[:, :, None]
    final_decay = running[length - 1]
    weights = jnp.exp(final_decay[None, :] - running) * step_part
    update = jnp.einsum('jhp,jn->hpn', x_part * weights[:, :, None], b_wide, precision=lax.Precision.HIGHEST)
    new_memory = memory * jnp.exp(final_decay)[:, None, None] + update
    return (new_memory, inside + earlier)

def reference(x_in, z_gate, b_in, c_in, dt_raw, a_log, d_skip, conv_x, conv_bc, norm_gain, w_out):
    rim_rows = conv_x.shape[0] - 1
    x_conv = causal_conv(x_in, jnp.zeros((rim_rows, x_in.shape[1]), jnp.bfloat16), conv_x)
    bc_in = jnp.concatenate([b_in, c_in], axis=1)
    bc_conv = causal_conv(bc_in, jnp.zeros((rim_rows, bc_in.shape[1]), jnp.bfloat16), conv_bc)
    b_conv = bc_conv[:, :STATE]
    c_conv = bc_conv[:, STATE:]
    dt_step = jax.nn.softplus(dt_raw)
    log_decay = -jnp.exp(a_log)[None, :] * dt_step
    x_heads = x_conv.astype(jnp.float32).reshape(FRAME_LENGTH, HEADS, HEAD_DIM)
    blocks = FRAME_LENGTH // SPAN

    def split_blocks(values):
        return values.reshape((blocks, SPAN) + values.shape[1:])
    start = jnp.zeros((HEADS, HEAD_DIM, STATE), jnp.float32)
    _, outputs = lax.scan(span_step, start, (split_blocks(x_heads), split_blocks(b_conv), split_blocks(c_conv), split_blocks(dt_step), split_blocks(log_decay)))
    ssd = outputs.reshape(FRAME_LENGTH, HEADS, HEAD_DIM) + d_skip[None, :, None] * x_heads
    gated = ssd.reshape(FRAME_LENGTH, INNER) * jax.nn.silu(z_gate.astype(jnp.float32))
    squares = lax.optimization_barrier(jnp.sum(gated * gated, axis=1))
    normed = (gated * lax.rsqrt(squares / INNER + 1e-05)[:, None] * norm_gain[None, :]).astype(jnp.bfloat16)
    group = INNER // N_HEAD

    def add_group(summed, index):
        piece = lax.dynamic_slice_in_dim(normed, index * group, group, 1)
        rows_w = lax.dynamic_slice_in_dim(w_out, index * group, group, 0)
        term = jnp.dot(piece, rows_w, preferred_element_type=jnp.float32).astype(jnp.bfloat16)
        term = lax.optimization_barrier(term)
        return (summed + term.astype(jnp.float32), None)
    summed, _ = lax.scan(add_group, jnp.zeros((FRAME_LENGTH, D), jnp.float32), jnp.arange(N_HEAD, dtype=jnp.int32))
    return summed.astype(jnp.bfloat16)
```

```python
import functools

import jax
import jax.numpy as jnp
from jax import lax
from jax.experimental import pallas as pl
from jax.experimental.pallas import tpu as pltpu
from jax.sharding import PartitionSpec as P


INNER = 8192
norm_eps = 1e-05
Q = 128
bf16 = jnp.bfloat16
f32 = jnp.float32


def silu(v):
    half = 0.5 * v
    return half + half * jnp.tanh(half)


def dot(a, b):
    return jnp.dot(a, b, preferred_element_type=f32)


def dot_t(a, b):
    return lax.dot_general(a, b, (((1,), (1,)), ((), ())), preferred_element_type=f32)


def head_column(ref, shape):
    rows = lax.broadcasted_iota(jnp.int32, shape, 0)
    out = jnp.full(shape, ref[0], f32)
    for h in range(1, 8):
        out = jnp.where(rows == h, ref[h], out)
    return out


def scan_kernel(
    a_ref, skip_ref, x_ref, b_ref, c_ref, rim_ref, dt_ref, wx_ref, wbc_ref,
    y_ref, cc_ref, cum_ref, msg_ref,
    xs, bs, st, tot,
):
    i = pl.program_id(0)

    @pl.when(i == 0)
    def _():
        xs[5:8, :] = rim_ref[:, :512].astype(f32)
        bs[5:8, :] = rim_ref[:, 512:].astype(f32)
        st[...] = jnp.zeros_like(st)
        tot[...] = jnp.zeros_like(tot)

    @pl.when(i > 0)
    def _():
        xs[0:8, :] = xs[Q : Q + 8, :]
        bs[0:8, :] = bs[Q : Q + 8, :]

    xs[8 : Q + 8, :] = x_ref[...].astype(f32)
    bs[8 : Q + 8, :128] = b_ref[...].astype(f32)
    bs[8 : Q + 8, 128:] = c_ref[...].astype(f32)

    def conv(buf, w_ref):
        total = w_ref[0:1, :] * buf[5 : Q + 5, :]
        for k in range(1, 4):
            total = total + w_ref[k : k + 1, :] * buf[5 + k : Q + 5 + k, :]
        return silu(total)

    xc = conv(xs, wx_ref).astype(bf16)
    bc = conv(bs, wbc_ref).astype(bf16)
    b = bc[:, :128]
    c = bc[:, 128:]
    cc_ref[...] = c

    raw = jnp.transpose(dt_ref[...])
    dt = jnp.maximum(raw, 0.0) + jnp.log1p(jnp.exp(-jnp.abs(raw)))
    run = -jnp.exp(head_column(a_ref, (8, Q))) * dt
    lane8 = lax.broadcasted_iota(jnp.int32, (8, Q), 1)
    shift = 1
    while shift < Q:
        run = run + jnp.where(lane8 >= shift, pltpu.roll(run, shift, 1), 0.0)
        shift *= 2
    fin = jnp.broadcast_to(run[:, Q - 1 : Q], (8, Q))
    run_t = jnp.transpose(run)
    late = jnp.exp(jnp.minimum(fin - run, 0.0)) * dt
    b_t = jnp.transpose(b.astype(f32))
    row = lax.broadcasted_iota(jnp.int32, (Q, Q), 0)
    col = lax.broadcasted_iota(jnp.int32, (Q, Q), 1)
    scores = jnp.where(row >= col, dot_t(c, b), 0.0)
    low = col < 64
    low1 = low[:1]
    inter = dot(c, st[...].astype(bf16))
    for p in range(4):
        h = 2 * p
        cols = slice(128 * p, 128 * p + 128)
        xp = xc[:, cols]
        xf = xp.astype(f32)
        xb = jnp.concatenate(
            [jnp.where(low, xf, 0.0).astype(bf16), jnp.where(low, 0.0, xf).astype(bf16)], axis=0
        )
        wide = [jnp.broadcast_to(run_t[:, h + k : h + k + 1], (Q, Q)) for k in (0, 1)]
        mix = [
            (
                jnp.exp(jnp.minimum(wide[k] - run[h + k : h + k + 1, :], 0.0))
                * scores
                * dt[h + k : h + k + 1, :]
            ).astype(bf16)
            for k in (0, 1)
        ]
        bw = [(b_t * late[h + k : h + k + 1, :]).astype(bf16) for k in (0, 1)]
        lhs = jnp.concatenate(
            [jnp.concatenate(mix, axis=1), jnp.concatenate(bw, axis=1)], axis=0
        )
        both = dot(lhs, xb)
        grow = jnp.exp(jnp.where(low, wide[0], wide[1]))
        skip = jnp.where(low1, skip_ref[h], skip_ref[h + 1])
        y_ref[:, cols] = both[:Q] + grow * inter[:, cols] + skip * xf
        end = jnp.exp(jnp.where(low1, fin[h : h + 1, :], fin[h + 1 : h + 2, :]))
        st[:, cols] = st[:, cols] * end + both[Q:]
    cum_ref[...] = tot[...] + run
    tot[...] = tot[...] + fin

    @pl.when(i == pl.num_programs(0) - 1)
    def _():
        total = tot[...]
        row16 = lax.broadcasted_iota(jnp.int32, (16, 128), 0)
        low16 = lax.broadcasted_iota(jnp.int32, (16, 128), 1) < 64
        for half in range(2):
            pair = []
            for k in (0, 1):
                h = 4 * half + 2 * k
                pair.append(jnp.where(low16, total[h : h + 1, :], total[h + 1 : h + 2, :]))
            high = [v.astype(bf16).astype(f32) for v in pair]
            rest = [v - u for v, u in zip(pair, high)]
            tile = jnp.where(
                row16 == 0, high[0],
                jnp.where(row16 == 1, high[1], jnp.where(row16 == 2, rest[0], rest[1])),
            ).astype(bf16)
            for group in range(8):
                j = 2 * group + half
                msg_ref[j, :, 0:256] = st[
                    16 * group : 16 * group + 16, 256 * half : 256 * half + 256
                ].astype(bf16)
                msg_ref[j, :, 256:384] = tile


def block_scan(x_in, b_in, c_in, rim, dt_raw, a_log, d_skip, conv_x, conv_bc):
    rows = lambda n: pl.BlockSpec((Q, n), lambda i: (i, 0))
    full = lambda *s: pl.BlockSpec(s, lambda i: (0,) * len(s))
    smem = pl.BlockSpec(memory_space=pltpu.SMEM)
    return pl.pallas_call(
        scan_kernel,
        grid=(1024 // Q,),
        in_specs=[
            smem, smem, rows(512), rows(128), rows(128), full(3, 768), rows(8),
            full(4, 512), full(4, 256),
        ],
        out_specs=[
            rows(512), rows(128), pl.BlockSpec((8, Q), lambda i: (0, i)), full(16, 16, 384),
        ],
        out_shape=[
            jax.ShapeDtypeStruct((1024, 512), f32),
            jax.ShapeDtypeStruct((1024, 128), bf16),
            jax.ShapeDtypeStruct((8, 1024), f32),
            jax.ShapeDtypeStruct((16, 16, 384), bf16),
        ],
        scratch_shapes=[
            pltpu.VMEM((Q + 8, 512), f32),
            pltpu.VMEM((Q + 8, 256), f32),
            pltpu.VMEM((128, 512), f32),
            pltpu.VMEM((8, Q), f32),
        ],
        name="block_scan",
    )(a_log, d_skip, x_in, b_in, c_in, rim, dt_raw, conv_x, conv_bc)


def prefix_kernel(in_ref, out_ref):
    acc = jnp.zeros((16, 256), f32)
    for j in range(16):
        out_ref[j] = acc.astype(bf16)
        if j < 15:
            t = in_ref[j, :, 256:384].astype(f32)
            decay = jnp.exp(
                jnp.concatenate([t[0:1] + t[2:3], t[1:2] + t[3:4]], axis=1)
            )
            acc = acc * decay + in_ref[j, :, 0:256].astype(f32)


def prefix(msg):
    return pl.pallas_call(
        prefix_kernel, out_shape=jax.ShapeDtypeStruct((16, 16, 256), bf16), name="prefix"
    )(msg)


def gate_kernel(y_ref, cc_ref, cum_ref, z_ref, sin_ref, gain_ref, g_ref, sq_ref, st):
    @pl.when(pl.program_id(0) == 0)
    def _():
        for j in range(16):
            group, half = j // 2, j % 2
            st[16 * group : 16 * group + 16, 256 * half : 256 * half + 256] = sin_ref[j]

    grow_t = jnp.transpose(jnp.exp(cum_ref[...]))
    low = lax.broadcasted_iota(jnp.int32, (Q, 128), 1) < 64
    carried = dot(cc_ref[...], st[...])
    squares = jnp.zeros((8, Q), f32)
    ones = jnp.ones((8, 128), bf16)
    for p in range(4):
        cols = slice(128 * p, 128 * p + 128)
        grow = jnp.where(
            low,
            jnp.broadcast_to(grow_t[:, 2 * p : 2 * p + 1], (Q, 128)),
            jnp.broadcast_to(grow_t[:, 2 * p + 1 : 2 * p + 2], (Q, 128)),
        )
        ssd = y_ref[:, cols] + grow * carried[:, cols]
        g = ssd * silu(z_ref[:, cols].astype(f32))
        squares = squares + dot_t(ones, (g * g).astype(bf16))
        g_ref[:, cols] = (g * gain_ref[:, cols]).astype(bf16)
    sq_ref[...] = squares


def gate(y, cc, cum, z_gate, incoming, gain):
    rows = lambda n: pl.BlockSpec((Q, n), lambda i: (i, 0))
    full = lambda *s: pl.BlockSpec(s, lambda i: (0,) * len(s))
    lanes = pl.BlockSpec((8, Q), lambda i: (0, i))
    return pl.pallas_call(
        gate_kernel,
        grid=(1024 // Q,),
        in_specs=[rows(512), rows(128), lanes, rows(512), full(16, 16, 256), full(1, 512)],
        out_specs=[rows(512), lanes],
        out_shape=[
            jax.ShapeDtypeStruct((1024, 512), bf16),
            jax.ShapeDtypeStruct((8, 1024), f32),
        ],
        scratch_shapes=[pltpu.VMEM((128, 512), bf16)],
        name="gate",
    )(y, cc, cum, z_gate, incoming, gain)


def project_kernel(axis, picks, g_ref, w_ref, o_ref):
    here = lax.axis_index("head")
    parts = []
    for a in picks:
        for k in range(4):
            mask = a * 4 + k if axis == 0 else k * 4 + a
            owner = jnp.bitwise_xor(here, mask)
            parts.append(g_ref[pl.ds(pl.multiple_of(owner * 64, 64), 64), :])
    o_ref[...] = dot(jnp.concatenate(parts, axis=0), w_ref[...]).astype(bf16)


def project(g, w_out, axis, picks, column):
    return pl.pallas_call(
        functools.partial(project_kernel, axis, picks),
        grid=(1,),
        in_specs=[
            pl.BlockSpec((1024, 512), lambda i: (0, 0)),
            pl.BlockSpec((512, 1024), lambda i: (0, column)),
        ],
        out_specs=pl.BlockSpec((512, 1024), lambda i: (0, 0)),
        out_shape=jax.ShapeDtypeStruct((512, 1024), bf16),
        name="project",
    )(g, w_out)


def swap(values, axis, mask):
    mask = mask * 4 if axis == 0 else mask
    return lax.ppermute(values, "head", [(h, h ^ mask) for h in range(16)])


def summed_to_owners(g, w_out):
    sets = ((0, 1, 0), (0, 3, 1), (1, 1, 2), (1, 3, 3))
    sent = [
        swap(project(g, w_out, ax, (m, 2), q), ax, m) for ax, m, q in sets
    ]
    kept = [project(g, w_out, ax, (0, m ^ 2), q) for ax, m, q in sets]
    state = []
    for (ax, m, q), own, got in zip(sets, kept, sent):
        total = (own.astype(f32) + got.astype(f32)).reshape(2, 4, 64, 1024)
        state.append((total[0], swap(total[1].astype(bf16), ax, m ^ 2)))
    later = []
    for (ax, m, q), (own, got) in zip(sets, state):
        total = own + got.astype(f32)
        away = jnp.stack([total[m], total[2]]).astype(bf16)
        later.append((total[0], total[m ^ 2], swap(away, 1 - ax, m)))
    last = []
    for (ax, m, q), (first, second, got) in zip(sets, later):
        last.append(
            (
                first + got[0].astype(f32),
                swap((second + got[1].astype(f32)).astype(bf16), 1 - ax, m ^ 2),
            )
        )
    return jnp.concatenate([own + got.astype(f32) for own, got in last], axis=1)


def local(x_in, z_gate, b_in, c_in, dt_raw, a_log, d_skip, conv_x, conv_bc, norm_gain, w_out):
    edge = jnp.concatenate([x_in[1021:], b_in[1021:], c_in[1021:]], axis=1)
    rim = lax.ppermute(edge, "seq", [(i, i + 1) for i in range(15)])
    y, cc, cum, msg = block_scan(
        x_in, b_in, c_in, rim, dt_raw, a_log, d_skip, conv_x, conv_bc
    )
    pieces = prefix(lax.all_to_all(msg, "seq", 0, 0))
    incoming = lax.all_to_all(pieces, "seq", 0, 0)
    g, squares = gate(y, cc, cum, z_gate, incoming, norm_gain[None, :])
    spread = lax.all_to_all(squares[0].reshape(16, 64), "head", 0, 0)
    scale = lax.rsqrt(jnp.sum(spread, axis=0) / INNER + norm_eps)
    return (summed_to_owners(g, w_out) * scale[:, None]).astype(bf16)


def solution(mesh):
    in_specs = (
        P("seq", "head"),
        P("seq", "head"),
        P("seq", None),
        P("seq", None),
        P("seq", "head"),
        P("head"),
        P("head"),
        P(None, "head"),
        P(),
        P("head"),
        P("head", None),
    )
    out_specs = P(("seq", "head"), None)
    return jax.shard_map(local, mesh=mesh, in_specs=in_specs, out_specs=out_specs, check_vma=False)
```

```python
import functools

import jax
import jax.numpy as jnp
from jax import lax
from jax.experimental import pallas as pl
from jax.experimental.pallas import tpu as pltpu
from jax.sharding import PartitionSpec as P


INNER = 8192
norm_eps = 1e-05
Q = 128
bf16 = jnp.bfloat16
f32 = jnp.float32


def silu(v):
    half = 0.5 * v
    return half + half * jnp.tanh(half)


def dot(a, b):
    return jnp.dot(a, b, preferred_element_type=f32)


def dot_t(a, b):
    return lax.dot_general(a, b, (((1,), (1,)), ((), ())), preferred_element_type=f32)


def head_column(ref, shape):
    rows = lax.broadcasted_iota(jnp.int32, shape, 0)
    out = jnp.full(shape, ref[0], f32)
    for h in range(1, 8):
        out = jnp.where(rows == h, ref[h], out)
    return out


def scan_kernel(
    a_ref, skip_ref, x_ref, b_ref, c_ref, rim_ref, dt_ref, wx_ref, wbc_ref,
    y_ref, cc_ref, cum_ref, msg_ref,
    xs, bs, st, tot,
):
    i = pl.program_id(0)

    @pl.when(i == 0)
    def _():
        xs[5:8, :] = rim_ref[:, :512].astype(f32)
        bs[5:8, :] = rim_ref[:, 512:].astype(f32)
        st[...] = jnp.zeros_like(st)
        tot[...] = jnp.zeros_like(tot)

    @pl.when(i > 0)
    def _():
        xs[0:8, :] = xs[Q : Q + 8, :]
        bs[0:8, :] = bs[Q : Q + 8, :]

    xs[8 : Q + 8, :] = x_ref[...].astype(f32)
    bs[8 : Q + 8, :128] = b_ref[...].astype(f32)
    bs[8 : Q + 8, 128:] = c_ref[...].astype(f32)

    def conv(buf, w_ref):
        total = w_ref[0:1, :] * buf[5 : Q + 5, :]
        for k in range(1, 4):
            total = total + w_ref[k : k + 1, :] * buf[5 + k : Q + 5 + k, :]
        return silu(total)

    xc = conv(xs, wx_ref).astype(bf16)
    bc = conv(bs, wbc_ref).astype(bf16)
    b = bc[:, :128]
    c = bc[:, 128:]
    cc_ref[...] = c

    raw = jnp.transpose(dt_ref[...])
    dt = jnp.maximum(raw, 0.0) + jnp.log1p(jnp.exp(-jnp.abs(raw)))
    run = -jnp.exp(head_column(a_ref, (8, Q))) * dt
    lane8 = lax.broadcasted_iota(jnp.int32, (8, Q), 1)
    shift = 1
    while shift < Q:
        run = run + jnp.where(lane8 >= shift, pltpu.roll(run, shift, 1), 0.0)
        shift *= 2
    fin = jnp.broadcast_to(run[:, Q - 1 : Q], (8, Q))
    run_t = jnp.transpose(run)
    late = jnp.exp(jnp.minimum(fin - run, 0.0)) * dt
    b_t = jnp.transpose(b.astype(f32))
    row = lax.broadcasted_iota(jnp.int32, (Q, Q), 0)
    col = lax.broadcasted_iota(jnp.int32, (Q, Q), 1)
    scores = jnp.where(row >= col, dot_t(c, b), 0.0)
    low = col < 64
    low1 = low[:1]
    inter = dot(c, st[...].astype(bf16))
    for p in range(4):
        h = 2 * p
        cols = slice(128 * p, 128 * p + 128)
        xp = xc[:, cols]
        xf = xp.astype(f32)
        xb = jnp.concatenate(
            [jnp.where(low, xf, 0.0).astype(bf16), jnp.where(low, 0.0, xf).astype(bf16)], axis=0
        )
        wide = [jnp.broadcast_to(run_t[:, h + k : h + k + 1], (Q, Q)) for k in (0, 1)]
        mix = [
            (
                jnp.exp(jnp.minimum(wide[k] - run[h + k : h + k + 1, :], 0.0))
                * scores
                * dt[h + k : h + k + 1, :]
            ).astype(bf16)
            for k in (0, 1)
        ]
        bw = [(b_t * late[h + k : h + k + 1, :]).astype(bf16) for k in (0, 1)]
        lhs = jnp.concatenate(
            [jnp.concatenate(mix, axis=1), jnp.concatenate(bw, axis=1)], axis=0
        )
        both = dot(lhs, xb)
        grow = jnp.exp(jnp.where(low, wide[0], wide[1]))
        skip = jnp.where(low1, skip_ref[h], skip_ref[h + 1])
        y_ref[:, cols] = both[:Q] + grow * inter[:, cols] + skip * xf
        end = jnp.exp(jnp.where(low1, fin[h : h + 1, :], fin[h + 1 : h + 2, :]))
        st[:, cols] = st[:, cols] * end + both[Q:]
    cum_ref[...] = tot[...] + run
    tot[...] = tot[...] + fin

    @pl.when(i == pl.num_programs(0) - 1)
    def _():
        total = tot[...]
        row16 = lax.broadcasted_iota(jnp.int32, (16, 128), 0)
        low16 = lax.broadcasted_iota(jnp.int32, (16, 128), 1) < 64
        for half in range(2):
            pair = []
            for k in (0, 1):
                h = 4 * half + 2 * k
                pair.append(jnp.where(low16, total[h : h + 1, :], total[h + 1 : h + 2, :]))
            high = [v.astype(bf16).astype(f32) for v in pair]
            rest = [v - u for v, u in zip(pair, high)]
            tile = jnp.where(
                row16 == 0, high[0],
                jnp.where(row16 == 1, high[1], jnp.where(row16 == 2, rest[0], rest[1])),
            ).astype(bf16)
            for group in range(8):
                j = 2 * group + half
                msg_ref[j, :, 0:256] = st[
                    16 * group : 16 * group + 16, 256 * half : 256 * half + 256
                ].astype(bf16)
                msg_ref[j, :, 256:384] = tile


def block_scan(x_in, b_in, c_in, rim, dt_raw, a_log, d_skip, conv_x, conv_bc):
    rows = lambda n: pl.BlockSpec((Q, n), lambda i: (i, 0))
    full = lambda *s: pl.BlockSpec(s, lambda i: (0,) * len(s))
    smem = pl.BlockSpec(memory_space=pltpu.SMEM)
    return pl.pallas_call(
        scan_kernel,
        grid=(1024 // Q,),
        in_specs=[
            smem, smem, rows(512), rows(128), rows(128), full(3, 768), rows(8),
            full(4, 512), full(4, 256),
        ],
        out_specs=[
            rows(512), rows(128), pl.BlockSpec((8, Q), lambda i: (0, i)), full(16, 16, 384),
        ],
        out_shape=[
            jax.ShapeDtypeStruct((1024, 512), f32),
            jax.ShapeDtypeStruct((1024, 128), bf16),
            jax.ShapeDtypeStruct((8, 1024), f32),
            jax.ShapeDtypeStruct((16, 16, 384), bf16),
        ],
        scratch_shapes=[
            pltpu.VMEM((Q + 8, 512), f32),
            pltpu.VMEM((Q + 8, 256), f32),
            pltpu.VMEM((128, 512), f32),
            pltpu.VMEM((8, Q), f32),
        ],
        name="block_scan",
    )(a_log, d_skip, x_in, b_in, c_in, rim, dt_raw, conv_x, conv_bc)


def prefix_kernel(in_ref, out_ref):
    acc = jnp.zeros((16, 256), f32)
    for j in range(16):
        out_ref[j] = acc.astype(bf16)
        if j < 15:
            t = in_ref[j, :, 256:384].astype(f32)
            decay = jnp.exp(
                jnp.concatenate([t[0:1] + t[2:3], t[1:2] + t[3:4]], axis=1)
            )
            acc = acc * decay + in_ref[j, :, 0:256].astype(f32)


def prefix(msg):
    return pl.pallas_call(
        prefix_kernel, out_shape=jax.ShapeDtypeStruct((16, 16, 256), bf16), name="prefix"
    )(msg)


SETS = ((0, 1, 0), (0, 3, 1), (1, 1, 2), (1, 3, 3))


def gathered(g_ref, here, axis, picks):
    parts = []
    for a in picks:
        for k in range(4):
            mask = a * 4 + k if axis == 0 else k * 4 + a
            owner = jnp.bitwise_xor(here, mask)
            parts.append(g_ref[pl.ds(pl.multiple_of(owner * 64, 64), 64), :])
    return jnp.concatenate(parts, axis=0)


def gate_kernel(
    y_ref, cc_ref, cum_ref, z_ref, sin_ref, gain_ref, w_ref,
    g_ref, sq_ref, s0, s1, s2, s3, st,
):
    i = pl.program_id(0)
    here = lax.axis_index("head")

    @pl.when(i == 0)
    def _():
        for j in range(16):
            group, half = j // 2, j % 2
            st[16 * group : 16 * group + 16, 256 * half : 256 * half + 256] = sin_ref[j]

    @pl.when(i < 8)
    def _():
        grow_t = jnp.transpose(jnp.exp(cum_ref[...]))
        low = lax.broadcasted_iota(jnp.int32, (Q, 128), 1) < 64
        carried = dot(cc_ref[...], st[...])
        squares = jnp.zeros((8, Q), f32)
        ones = jnp.ones((8, 128), bf16)
        rows = pl.ds(pl.multiple_of(i * Q, Q), Q)
        for p in range(4):
            cols = slice(128 * p, 128 * p + 128)
            grow = jnp.where(
                low,
                jnp.broadcast_to(grow_t[:, 2 * p : 2 * p + 1], (Q, 128)),
                jnp.broadcast_to(grow_t[:, 2 * p + 1 : 2 * p + 2], (Q, 128)),
            )
            ssd = y_ref[:, cols] + grow * carried[:, cols]
            g = ssd * silu(z_ref[:, cols].astype(f32))
            squares = squares + dot_t(ones, (g * g).astype(bf16))
            g_ref[rows, cols] = (g * gain_ref[:, cols]).astype(bf16)
        sq_ref[...] = squares

    for q, (ax, m, _) in enumerate(SETS):

        @pl.when(i == 8 + q)
        def _(out=(s0, s1, s2, s3)[q], ax=ax, m=m):
            out[...] = dot(gathered(g_ref, here, ax, (m, 2)), w_ref[...]).astype(bf16)


def gate(y, cc, cum, z_gate, incoming, gain, w_out):
    row = lambda i: jnp.minimum(i, 7)
    rows = lambda n: pl.BlockSpec((Q, n), lambda i: (row(i), 0))
    full = lambda *s: pl.BlockSpec(s, lambda i: (0,) * len(s))
    lanes = pl.BlockSpec((8, Q), lambda i: (0, row(i)))
    return pl.pallas_call(
        gate_kernel,
        grid=(12,),
        in_specs=[
            rows(512), rows(128), lanes, rows(512), full(16, 16, 256), full(1, 512),
            pl.BlockSpec((512, 1024), lambda i: (0, jnp.maximum(i - 8, 0))),
        ],
        out_specs=[full(1024, 512), lanes] + [full(512, 1024)] * 4,
        out_shape=[
            jax.ShapeDtypeStruct((1024, 512), bf16),
            jax.ShapeDtypeStruct((8, 1024), f32),
        ]
        + [jax.ShapeDtypeStruct((512, 1024), bf16)] * 4,
        scratch_shapes=[pltpu.VMEM((128, 512), bf16)],
        name="gate",
    )(y, cc, cum, z_gate, incoming, gain, w_out)


def keep_kernel(g_ref, w_ref, k0, k1, k2, k3):
    i = pl.program_id(0)
    here = lax.axis_index("head")
    for q, (ax, m, _) in enumerate(SETS):

        @pl.when(i == q)
        def _(out=(k0, k1, k2, k3)[q], ax=ax, m=m):
            out[...] = dot(gathered(g_ref, here, ax, (0, m ^ 2)), w_ref[...]).astype(bf16)


def keep(g, w_out):
    full = lambda *s: pl.BlockSpec(s, lambda i: (0,) * len(s))
    return pl.pallas_call(
        keep_kernel,
        grid=(4,),
        in_specs=[full(1024, 512), pl.BlockSpec((512, 1024), lambda i: (0, i))],
        out_specs=[full(512, 1024)] * 4,
        out_shape=[jax.ShapeDtypeStruct((512, 1024), bf16)] * 4,
        name="keep",
    )(g, w_out)


def swap(values, axis, mask):
    mask = mask * 4 if axis == 0 else mask
    return lax.ppermute(values, "head", [(h, h ^ mask) for h in range(16)])


def summed_to_owners(sends, kept):
    sets = SETS
    sent = [swap(v, ax, m) for v, (ax, m, q) in zip(sends, sets)]
    state = []
    for (ax, m, q), own, got in zip(sets, kept, sent):
        total = (own.astype(f32) + got.astype(f32)).reshape(2, 4, 64, 1024)
        state.append((total[0], swap(total[1].astype(bf16), ax, m ^ 2)))
    later = []
    for (ax, m, q), (own, got) in zip(sets, state):
        total = own + got.astype(f32)
        away = jnp.stack([total[m], total[2]]).astype(bf16)
        later.append((total[0], total[m ^ 2], swap(away, 1 - ax, m)))
    last = []
    for (ax, m, q), (first, second, got) in zip(sets, later):
        last.append(
            (
                first + got[0].astype(f32),
                swap((second + got[1].astype(f32)).astype(bf16), 1 - ax, m ^ 2),
            )
        )
    return jnp.concatenate([own + got.astype(f32) for own, got in last], axis=1)


def local(x_in, z_gate, b_in, c_in, dt_raw, a_log, d_skip, conv_x, conv_bc, norm_gain, w_out):
    edge = jnp.concatenate([x_in[1021:], b_in[1021:], c_in[1021:]], axis=1)
    rim = lax.ppermute(edge, "seq", [(i, i + 1) for i in range(15)])
    y, cc, cum, msg = block_scan(
        x_in, b_in, c_in, rim, dt_raw, a_log, d_skip, conv_x, conv_bc
    )
    pieces = prefix(lax.all_to_all(msg, "seq", 0, 0))
    incoming = lax.all_to_all(pieces, "seq", 0, 0)
    g, squares, *sends = gate(
        y, cc, cum, z_gate, incoming, norm_gain[None, :], w_out
    )
    kept = keep(g, w_out)
    squares, *kept = lax.optimization_barrier((squares, *kept))
    spread = lax.all_to_all(squares[0].reshape(16, 64), "head", 0, 0)
    scale = lax.rsqrt(jnp.sum(spread, axis=0) / INNER + norm_eps)
    return (summed_to_owners(sends, kept) * scale[:, None]).astype(bf16)


def solution(mesh):
    in_specs = (
        P("seq", "head"),
        P("seq", "head"),
        P("seq", None),
        P("seq", None),
        P("seq", "head"),
        P("head"),
        P("head"),
        P(None, "head"),
        P(),
        P("head"),
        P("head", None),
    )
    out_specs = P(("seq", "head"), None)
    return jax.shard_map(local, mesh=mesh, in_specs=in_specs, out_specs=out_specs, check_vma=False)
```

```python
import jax
import jax.numpy as jnp
from jax import lax
from jax.experimental import pallas as pl
from jax.experimental.pallas import tpu as pltpu
from jax.sharding import PartitionSpec as P


INNER = 8192
norm_eps = 1e-05
Q = 128
bf16 = jnp.bfloat16
f32 = jnp.float32


def silu(v):
    half = 0.5 * v
    return half + half * jnp.tanh(half)


def dot(a, b):
    return jnp.dot(a, b, preferred_element_type=f32)


def dot_t(a, b):
    return lax.dot_general(a, b, (((1,), (1,)), ((), ())), preferred_element_type=f32)


def head_column(ref, shape):
    rows = lax.broadcasted_iota(jnp.int32, shape, 0)
    out = jnp.full(shape, ref[0], f32)
    for h in range(1, 8):
        out = jnp.where(rows == h, ref[h], out)
    return out


def edge_kernel(x_ref, b_ref, c_ref, o_ref):
    o_ref[:, :512] = x_ref[...]
    o_ref[:, 512:640] = b_ref[...]
    o_ref[:, 640:] = c_ref[...]


def edge_rows(x_in, b_in, c_in):
    last = lambda n: pl.BlockSpec((16, n), lambda i: (63, 0))
    return pl.pallas_call(
        edge_kernel,
        grid=(1,),
        in_specs=[last(512), last(128), last(128)],
        out_specs=pl.BlockSpec((16, 768), lambda i: (0, 0)),
        out_shape=jax.ShapeDtypeStruct((16, 768), bf16),
        name="edge",
    )(x_in, b_in, c_in)


def pair_row(low, values, h):
    return jnp.where(low, values[h : h + 1, :], values[h + 1 : h + 2, :])


def decay_kernel(a_ref, dt_ref, run_ref, step_ref, late_ref, grow_ref):
    rate = -jnp.exp(head_column(a_ref, (8, Q)))
    lane8 = lax.broadcasted_iota(jnp.int32, (8, Q), 1)

    def halves(v):
        high = v.astype(bf16).astype(f32)
        return jnp.transpose(jnp.concatenate([high, v - high], axis=0)).astype(bf16)

    for i in range(1024 // Q):
        lanes = slice(i * Q, i * Q + Q)
        raw = dt_ref[:, lanes]
        dt = jnp.maximum(raw, 0.0) + jnp.log1p(jnp.exp(-jnp.abs(raw)))
        run = rate * dt
        shift = 1
        while shift < Q:
            run = run + jnp.where(lane8 >= shift, pltpu.roll(run, shift, 1), 0.0)
            shift *= 2
        fin = jnp.broadcast_to(run[:, Q - 1 : Q], (8, Q))
        run_ref[:, lanes] = run
        step_ref[:, lanes] = dt
        late_ref[lanes, :] = halves(jnp.exp(jnp.minimum(fin - run, 0.0)) * dt)
        grow_ref[lanes, :] = halves(jnp.exp(run))


def decays(dt_raw, a_log):
    full = lambda *s: pl.BlockSpec(s, lambda i: (0,) * len(s))
    return pl.pallas_call(
        decay_kernel,
        grid=(1,),
        in_specs=[pl.BlockSpec(memory_space=pltpu.SMEM), full(8, 1024)],
        out_specs=[full(8, 1024)] * 2 + [full(1024, 16)] * 2,
        out_shape=[jax.ShapeDtypeStruct((8, 1024), f32)] * 2
        + [jax.ShapeDtypeStruct((1024, 16), bf16)] * 2,
        name="decays",
    )(a_log, dt_raw.T)


def spread():
    lane = lax.broadcasted_iota(jnp.int32, (16, 512), 1)
    row = lax.broadcasted_iota(jnp.int32, (16, 512), 0)
    first = jnp.where(row >= 8, row - 8, row) * 64
    return jnp.where((lane >= first) & (lane < first + 64), 1.0, 0.0).astype(bf16)


def state_kernel(
    x_ref, b_ref, c_ref, rim_ref, run_ref, late_ref, wx_ref, wbc_ref,
    xc_ref, bc_ref, before_ref, states_ref, msg_ref,
    xs, bs, st, tot,
):
    i = pl.program_id(0)

    @pl.when(i == 0)
    def _():
        xs[0:8, :] = rim_ref[8:16, :512].astype(f32)
        bs[0:8, :] = rim_ref[8:16, 512:].astype(f32)
        st[...] = jnp.zeros_like(st)
        tot[...] = jnp.zeros_like(tot)

    @pl.when(i > 0)
    def _():
        xs[0:8, :] = xs[Q : Q + 8, :]
        bs[0:8, :] = bs[Q : Q + 8, :]

    xs[8 : Q + 8, :] = x_ref[...].astype(f32)
    bs[8 : Q + 8, :128] = b_ref[...].astype(f32)
    bs[8 : Q + 8, 128:] = c_ref[...].astype(f32)

    def conv(buf, w_ref, cols):
        whole = buf[:, cols]
        half = 0.5 * w_ref[:, cols]
        total = half[3:4] * whole[8:]
        for k in range(3):
            total = total + half[k : k + 1] * pltpu.roll(whole, 3 - k, 0)[8:]
        return total + total * jnp.tanh(total)

    fin = jnp.broadcast_to(run_ref[:, Q - 1 : Q], (8, 128))
    b = conv(bs, wbc_ref, slice(0, 128))
    bc_ref[:, :128] = b.astype(bf16)
    bc_ref[:, 128:] = conv(bs, wbc_ref, slice(128, 256)).astype(bf16)
    b_t = jnp.transpose(b).astype(bf16)
    low1 = lax.broadcasted_iota(jnp.int32, (1, 128), 1) < 64
    late = dot(late_ref[...], spread())
    states_ref[...] = st[...].astype(bf16)
    before_ref[...] = tot[...]
    for p in range(4):
        cols = slice(128 * p, 128 * p + 128)
        xp = conv(xs, wx_ref, cols)
        xc_ref[:, cols] = xp.astype(bf16)
        end = jnp.exp(pair_row(low1, fin, 2 * p))
        st[:, cols] = st[:, cols] * end + dot(b_t, (xp * late[:, cols]).astype(bf16))
    tot[...] = tot[...] + fin

    @pl.when(i == pl.num_programs(0) - 1)
    def _():
        total = tot[...]
        row8 = lax.broadcasted_iota(jnp.int32, (8, 128), 0)
        for p in range(4):
            decay = jnp.broadcast_to(pair_row(low1, total, 2 * p), (8, 128))
            high = decay.astype(bf16).astype(f32)
            tile = jnp.where(row8 == 0, high, decay - high).astype(bf16)
            for group in range(4):
                j = 4 * group + p
                msg_ref[j, 0:32, :] = st[
                    32 * group : 32 * group + 32, 128 * p : 128 * p + 128
                ].astype(bf16)
                msg_ref[j, 32:40, :] = tile


def block_states(x_in, b_in, c_in, rim, run, late, conv_x, conv_bc):
    rows = lambda n: pl.BlockSpec((Q, n), lambda i: (i, 0))
    full = lambda *s: pl.BlockSpec(s, lambda i: (0,) * len(s))
    lanes = pl.BlockSpec((8, Q), lambda i: (0, i))
    return pl.pallas_call(
        state_kernel,
        grid=(1024 // Q,),
        in_specs=[
            rows(512), rows(128), rows(128), full(16, 768), lanes, rows(16),
            full(4, 512), full(4, 256),
        ],
        out_specs=[rows(512), rows(256), lanes, rows(512), full(16, 40, 128)],
        out_shape=[
            jax.ShapeDtypeStruct((1024, 512), bf16),
            jax.ShapeDtypeStruct((1024, 256), bf16),
            jax.ShapeDtypeStruct((8, 1024), f32),
            jax.ShapeDtypeStruct((1024, 512), bf16),
            jax.ShapeDtypeStruct((16, 40, 128), bf16),
        ],
        scratch_shapes=[
            pltpu.VMEM((Q + 8, 512), f32),
            pltpu.VMEM((Q + 8, 256), f32),
            pltpu.VMEM((128, 512), f32),
            pltpu.VMEM((8, Q), f32),
        ],
        name="states",
    )(x_in, b_in, c_in, rim, run, late, conv_x, conv_bc)


def inside_kernel(skip_ref, xc_ref, bc_ref, run_ref, step_ref, y_ref):
    b = bc_ref[:, :128]
    c = bc_ref[:, 128:]
    run = run_ref[...]
    dt = step_ref[...]
    run_t = jnp.transpose(run)
    row = lax.broadcasted_iota(jnp.int32, (Q, Q), 0)
    col = lax.broadcasted_iota(jnp.int32, (Q, Q), 1)
    scores = jnp.where(row >= col, dot_t(c, b), 0.0)
    low = col < 64
    for p in range(4):
        h = 2 * p
        cols = slice(128 * p, 128 * p + 128)
        xf = xc_ref[:, cols].astype(f32)
        xb = jnp.concatenate(
            [jnp.where(low, xf, 0.0).astype(bf16), jnp.where(low, 0.0, xf).astype(bf16)], axis=0
        )
        mix = []
        for k in (h, h + 1):
            fade = jnp.exp(jnp.minimum(run_t[:, k : k + 1] - run[k : k + 1, :], 0.0))
            mix.append((fade * scores * dt[k : k + 1, :]).astype(bf16))
        skip = jnp.where(low[:1], skip_ref[h], skip_ref[h + 1])
        y_ref[:, cols] = dot(jnp.concatenate(mix, axis=1), xb) + skip * xf


def inside(xc, bc, run, step, d_skip):
    rows = lambda n: pl.BlockSpec((Q, n), lambda i: (i, 0))
    lanes = pl.BlockSpec((8, Q), lambda i: (0, i))
    return pl.pallas_call(
        inside_kernel,
        grid=(1024 // Q,),
        in_specs=[
            pl.BlockSpec(memory_space=pltpu.SMEM), rows(512), rows(256), lanes, lanes,
        ],
        out_specs=rows(512),
        out_shape=jax.ShapeDtypeStruct((1024, 512), f32),
        name="inside",
    )(d_skip, xc, bc, run, step)


def prefix_kernel(in_ref, out_ref):
    acc = jnp.zeros((32, 128), f32)
    for j in range(16):
        out_ref[j] = acc.astype(bf16)
        if j < 15:
            t = in_ref[j, 32:40, :].astype(f32)
            decay = jnp.exp(t[0:1] + t[1:2])
            acc = acc * decay + in_ref[j, 0:32, :].astype(f32)


def prefix(msg):
    return pl.pallas_call(
        prefix_kernel, out_shape=jax.ShapeDtypeStruct((16, 32, 128), bf16), name="prefix"
    )(msg)


SETS = ((0, 1, 0), (0, 3, 1), (1, 1, 2), (1, 3, 3))
WIDTHS = (1152, 1024, 1024, 1024)


def projected(g_ref, w_ref, out, here, axis, picks):
    parts = []
    for pick in picks:
        for k in range(4):
            mask = pick * 4 + k if axis == 0 else k * 4 + pick
            owner = jnp.bitwise_xor(here, mask)
            parts.append(g_ref[pl.ds(pl.multiple_of(owner * 64, 64), 64), :])
    rows = jnp.concatenate(parts, axis=0)
    out[:, :1024] = dot(rows[:, :512], w_ref[...]).astype(bf16)
    if out.shape[1] > 1024:
        out[:, 1024:] = rows[:, 512:]


def gate_kernel(
    y_ref, bc_ref, grow_ref, before_ref, states_ref, z_ref, sin_ref, gain_ref, w_ref,
    *rest,
):
    outs, (st, g, b0, b1, b2, b3, sems) = rest[:9], rest[9:]
    i = pl.program_id(0)
    here = lax.axis_index("head")
    bufs = (b0, b1, b2, b3)

    def out_copy(n):
        if n == 8:
            return pltpu.make_async_copy(g, outs[8], sems.at[8])
        q, part = n % 4, n // 4
        return pltpu.make_async_copy(
            bufs[q].at[part * 256 : part * 256 + 256], outs[n], sems.at[n]
        )

    @pl.when(i == 0)
    def _():
        for j in range(16):
            group, p = j // 4, j % 4
            st[32 * group : 32 * group + 32, 128 * p : 128 * p + 128] = sin_ref[j].astype(f32)

    @pl.when(i < 8)
    def _():
        before = jnp.exp(before_ref[...])
        low1 = lax.broadcasted_iota(jnp.int32, (1, 128), 1) < 64
        grow = dot(grow_ref[...], spread())
        c = bc_ref[:, 128:]
        squares = jnp.zeros((Q, 128), f32)
        rows = pl.ds(pl.multiple_of(i * Q, Q), Q)
        for p in range(4):
            cols = slice(128 * p, 128 * p + 128)
            entering = states_ref[:, cols].astype(f32) + st[:, cols] * pair_row(
                low1, before, 2 * p
            )
            ssd = y_ref[:, cols] + grow[:, cols] * dot(c, entering.astype(bf16))
            v = ssd * silu(z_ref[:, cols].astype(f32))
            squares = squares + v * v
            g[rows, cols] = (v * gain_ref[:, cols]).astype(bf16)
        g[rows, 512:] = dot(squares.astype(bf16), jnp.ones((128, 128), bf16)).astype(bf16)

    for q, (ax, m, _) in enumerate(SETS):

        @pl.when(i == 8 + q)
        def _(q=q, ax=ax, m=m):
            projected(g, w_ref, bufs[q], here, ax, (2, m))
            out_copy(q).start()
            out_copy(4 + q).start()

    @pl.when(i == 8)
    def _():
        out_copy(8).start()

    @pl.when(i == 11)
    def _():
        for n in range(9):
            out_copy(n).wait()


def gate(y, bc, grow, before, states, z_gate, incoming, gain, w_out):
    row = lambda i: jnp.minimum(i, 7)
    rows = lambda n: pl.BlockSpec((Q, n), lambda i: (row(i), 0))
    full = lambda *s: pl.BlockSpec(s, lambda i: (0,) * len(s))
    lanes = pl.BlockSpec((8, Q), lambda i: (0, row(i)))
    return pl.pallas_call(
        gate_kernel,
        grid=(12,),
        in_specs=[
            rows(512), rows(256), rows(16), lanes, rows(512), rows(512), full(16, 32, 128),
            full(1, 512), pl.BlockSpec((512, 1024), lambda i: (0, jnp.maximum(i - 8, 0))),
        ],
        out_specs=[pl.BlockSpec(memory_space=pl.ANY)] * 9,
        out_shape=[jax.ShapeDtypeStruct((256, n), bf16) for n in WIDTHS * 2]
        + [jax.ShapeDtypeStruct((1024, 640), bf16)],
        scratch_shapes=[pltpu.VMEM((128, 512), f32), pltpu.VMEM((1024, 640), bf16)]
        + [pltpu.VMEM((512, n), bf16) for n in WIDTHS]
        + [pltpu.SemaphoreType.DMA((9,))],
        name="gate",
    )(y, bc, grow, before, states, z_gate, incoming, gain, w_out)


def keep_kernel(g_ref, w_ref, *rest):
    outs, (b0, b1, b2, b3, sems) = rest[:8], rest[8:]
    bufs = (b0, b1, b2, b3)
    i = pl.program_id(0)
    here = lax.axis_index("head")

    def out_copy(n):
        q, part = n % 4, n // 4
        return pltpu.make_async_copy(
            bufs[q].at[part * 256 : part * 256 + 256], outs[n], sems.at[n]
        )

    for q, (ax, m, _) in enumerate(SETS):

        @pl.when(i == q)
        def _(q=q, ax=ax, m=m):
            projected(g_ref, w_ref, bufs[q], here, ax, (m ^ 2, 0))
            out_copy(q).start()
            out_copy(4 + q).start()

    @pl.when(i == 3)
    def _():
        for n in range(8):
            out_copy(n).wait()


def keep(g, w_out):
    return pl.pallas_call(
        keep_kernel,
        grid=(4,),
        in_specs=[
            pl.BlockSpec((1024, 640), lambda i: (0, 0)),
            pl.BlockSpec((512, 1024), lambda i: (0, i)),
        ],
        out_specs=[pl.BlockSpec(memory_space=pl.ANY)] * 8,
        out_shape=[jax.ShapeDtypeStruct((256, n), bf16) for n in WIDTHS * 2],
        scratch_shapes=[pltpu.VMEM((512, n), bf16) for n in WIDTHS]
        + [pltpu.SemaphoreType.DMA((8,))],
        name="keep",
    )(g, w_out)


def swap(values, axis, mask):
    mask = mask * 4 if axis == 0 else mask
    return lax.ppermute(values, "head", [(h, h ^ mask) for h in range(16)])


def added(*values):
    total = values[0].astype(f32)
    for v in values[1:]:
        total = total + v.astype(f32)
    return total


def summed_to_owners(g, sends, w_out):
    far = []
    for q, (ax, m, _) in enumerate(SETS):
        far.append(swap(sends[q], ax, m))
    near = []
    for q, (ax, m, _) in enumerate(SETS):
        near.append(swap(sends[4 + q], ax, m))
    kept = keep(g, w_out)
    passed, own = kept[:4], kept[4:]
    second = [
        swap(added(a, b).astype(bf16), ax, m ^ 2) for a, b, (ax, m, q) in zip(passed, far, SETS)
    ]
    later = []
    for (ax, m, q), a, b, c in zip(SETS, own, near, second):
        total = added(a, b, c).reshape(4, 64, -1)
        away = jnp.stack([total[m], total[2]]).astype(bf16)
        later.append((total[0], total[m ^ 2], swap(away, 1 - ax, m)))
    last = []
    for (ax, m, q), (first, second, got) in zip(SETS, later):
        last.append(
            (
                added(first, got[0]),
                swap(added(second, got[1]).astype(bf16), 1 - ax, m ^ 2),
            )
        )
    parts = [added(a, b) for a, b in last]
    scale = lax.rsqrt(parts[0][:, 1024:1025] / INNER + norm_eps)
    return jnp.concatenate([v[:, :1024] * scale for v in parts], axis=1).astype(bf16)


def layer(x_in, z_gate, b_in, c_in, dt_raw, a_log, d_skip, conv_x, conv_bc, norm_gain, w_out):
    rim = lax.ppermute(
        edge_rows(x_in, b_in, c_in), "seq", [(i, i + 1) for i in range(15)]
    )
    run, step, late, grow = decays(dt_raw, a_log)
    xc, bc, before, states, msg = block_states(
        x_in, b_in, c_in, rim, run, late, conv_x, conv_bc
    )
    pieces = prefix(lax.all_to_all(msg, "seq", 0, 0))
    incoming = lax.all_to_all(pieces, "seq", 0, 0)
    y = inside(xc, bc, run, step, d_skip)
    *sends, g = gate(
        y, bc, grow, before, states, z_gate, incoming, norm_gain[None, :], w_out
    )
    return summed_to_owners(g, sends, w_out)


def solution(mesh):
    in_specs = (
        P("seq", "head"),
        P("seq", "head"),
        P("seq", None),
        P("seq", None),
        P("seq", "head"),
        P("head"),
        P("head"),
        P(None, "head"),
        P(),
        P("head"),
        P("head", None),
    )
    out_specs = P(("seq", "head"), None)
    return jax.shard_map(
        layer, mesh=mesh, in_specs=in_specs, out_specs=out_specs, check_vma=False
    )
```

```python
import jax
import jax.numpy as jnp
from jax import lax
from jax.experimental import pallas as pl
from jax.experimental.pallas import tpu as pltpu
from jax.sharding import PartitionSpec as P


INNER = 8192
norm_eps = 1e-05
Q = 128
PARAMS = pltpu.CompilerParams(vmem_limit_bytes=24 * 2**20)
bf16 = jnp.bfloat16
f32 = jnp.float32


def in_hbm(v):
    return pltpu.with_memory_space_constraint(v, pltpu.HBM)


def silu(v):
    half = 0.5 * v
    return half + half * jnp.tanh(half)


def dot(a, b):
    return jnp.dot(a, b, preferred_element_type=f32)


def dot_t(a, b):
    return lax.dot_general(a, b, (((1,), (1,)), ((), ())), preferred_element_type=f32)


def head_column(ref, shape):
    rows = lax.broadcasted_iota(jnp.int32, shape, 0)
    out = jnp.full(shape, ref[0], f32)
    for h in range(1, 8):
        out = jnp.where(rows == h, ref[h], out)
    return out


def edge_kernel(x_ref, b_ref, c_ref, o_ref):
    o_ref[:, :512] = x_ref[...]
    o_ref[:, 512:640] = b_ref[...]
    o_ref[:, 640:] = c_ref[...]


def edge_rows(x_in, b_in, c_in):
    last = lambda n: pl.BlockSpec((16, n), lambda i: (63, 0))
    return pl.pallas_call(
        edge_kernel,
        grid=(1,),
        in_specs=[last(512), last(128), last(128)],
        out_specs=pl.BlockSpec((16, 768), lambda i: (0, 0)),
        out_shape=jax.ShapeDtypeStruct((16, 768), bf16),
        name="edge",
        compiler_params=PARAMS,
    )(in_hbm(x_in), in_hbm(b_in), in_hbm(c_in))


def pair_row(low, values, h):
    return jnp.where(low, values[h : h + 1, :], values[h + 1 : h + 2, :])


def decay_kernel(a_ref, dt_ref, run_ref, step_ref, late_ref, grow_ref):
    rate = -jnp.exp(head_column(a_ref, (8, Q)))
    lane8 = lax.broadcasted_iota(jnp.int32, (8, Q), 1)

    def halves(v):
        high = v.astype(bf16).astype(f32)
        return jnp.transpose(jnp.concatenate([high, v - high], axis=0)).astype(bf16)

    for i in range(1024 // Q):
        lanes = slice(i * Q, i * Q + Q)
        raw = dt_ref[:, lanes]
        dt = jnp.maximum(raw, 0.0) + jnp.log1p(jnp.exp(-jnp.abs(raw)))
        run = rate * dt
        shift = 1
        while shift < Q:
            run = run + jnp.where(lane8 >= shift, pltpu.roll(run, shift, 1), 0.0)
            shift *= 2
        fin = jnp.broadcast_to(run[:, Q - 1 : Q], (8, Q))
        run_ref[:, lanes] = run
        step_ref[:, lanes] = dt
        late_ref[lanes, :] = halves(jnp.exp(jnp.minimum(fin - run, 0.0)) * dt)
        grow_ref[lanes, :] = halves(jnp.exp(run))


def decays(dt_raw, a_log):
    full = lambda *s: pl.BlockSpec(s, lambda i: (0,) * len(s))
    return pl.pallas_call(
        decay_kernel,
        grid=(1,),
        in_specs=[pl.BlockSpec(memory_space=pltpu.SMEM), full(8, 1024)],
        out_specs=[full(8, 1024)] * 2 + [full(1024, 16)] * 2,
        out_shape=[jax.ShapeDtypeStruct((8, 1024), f32)] * 2
        + [jax.ShapeDtypeStruct((1024, 16), bf16)] * 2,
        name="decays",
        compiler_params=PARAMS,
    )(a_log, dt_raw.T)


def spread():
    lane = lax.broadcasted_iota(jnp.int32, (16, 512), 1)
    row = lax.broadcasted_iota(jnp.int32, (16, 512), 0)
    first = jnp.where(row >= 8, row - 8, row) * 64
    return jnp.where((lane >= first) & (lane < first + 64), 1.0, 0.0).astype(bf16)


def state_kernel(
    x_ref, b_ref, c_ref, rim_ref, run_ref, late_ref, wx_ref, wbc_ref,
    xc_ref, bc_ref, before_ref, states_ref, msg_ref,
    xs, bs, st, tot,
):
    i = pl.program_id(0)

    @pl.when(i == 0)
    def _():
        xs[0:8, :] = rim_ref[8:16, :512].astype(f32)
        bs[0:8, :] = rim_ref[8:16, 512:].astype(f32)
        st[...] = jnp.zeros_like(st)
        tot[...] = jnp.zeros_like(tot)

    @pl.when(i > 0)
    def _():
        xs[0:8, :] = xs[Q : Q + 8, :]
        bs[0:8, :] = bs[Q : Q + 8, :]

    xs[8 : Q + 8, :] = x_ref[...].astype(f32)
    bs[8 : Q + 8, :128] = b_ref[...].astype(f32)
    bs[8 : Q + 8, 128:] = c_ref[...].astype(f32)

    def conv(buf, w_ref, cols):
        whole = buf[:, cols]
        half = 0.5 * w_ref[:, cols]
        total = half[3:4] * whole[8:]
        for k in range(3):
            total = total + half[k : k + 1] * pltpu.roll(whole, 3 - k, 0)[8:]
        return total + total * jnp.tanh(total)

    fin = jnp.broadcast_to(run_ref[:, Q - 1 : Q], (8, 128))
    b = conv(bs, wbc_ref, slice(0, 128))
    bc_ref[:, :128] = b.astype(bf16)
    bc_ref[:, 128:] = conv(bs, wbc_ref, slice(128, 256)).astype(bf16)
    b_t = jnp.transpose(b).astype(bf16)
    low1 = lax.broadcasted_iota(jnp.int32, (1, 128), 1) < 64
    late = dot(late_ref[...], spread())
    states_ref[...] = st[...].astype(bf16)
    before_ref[...] = tot[...]
    for p in range(4):
        cols = slice(128 * p, 128 * p + 128)
        xp = conv(xs, wx_ref, cols)
        xc_ref[:, cols] = xp.astype(bf16)
        end = jnp.exp(pair_row(low1, fin, 2 * p))
        st[:, cols] = st[:, cols] * end + dot(b_t, (xp * late[:, cols]).astype(bf16))
    tot[...] = tot[...] + fin

    @pl.when(i == pl.num_programs(0) - 1)
    def _():
        total = tot[...]
        row8 = lax.broadcasted_iota(jnp.int32, (8, 128), 0)
        for p in range(4):
            decay = jnp.broadcast_to(pair_row(low1, total, 2 * p), (8, 128))
            high = decay.astype(bf16).astype(f32)
            tile = jnp.where(row8 == 0, high, decay - high).astype(bf16)
            for group in range(4):
                j = 4 * group + p
                msg_ref[j, 0:32, :] = st[
                    32 * group : 32 * group + 32, 128 * p : 128 * p + 128
                ].astype(bf16)
                msg_ref[j, 32:40, :] = tile


def block_states(x_in, b_in, c_in, rim, run, late, conv_x, conv_bc):
    rows = lambda n: pl.BlockSpec((Q, n), lambda i: (i, 0))
    full = lambda *s: pl.BlockSpec(s, lambda i: (0,) * len(s))
    lanes = pl.BlockSpec((8, Q), lambda i: (0, i))
    return pl.pallas_call(
        state_kernel,
        grid=(1024 // Q,),
        in_specs=[
            rows(512), rows(128), rows(128), full(16, 768), lanes, rows(16),
            full(4, 512), full(4, 256),
        ],
        out_specs=[rows(512), rows(256), lanes, rows(512), full(16, 40, 128)],
        out_shape=[
            pltpu.HBM((1024, 512), bf16),
            jax.ShapeDtypeStruct((1024, 256), bf16),
            jax.ShapeDtypeStruct((8, 1024), f32),
            pltpu.HBM((1024, 512), bf16),
            jax.ShapeDtypeStruct((16, 40, 128), bf16),
        ],
        scratch_shapes=[
            pltpu.VMEM((Q + 8, 512), f32),
            pltpu.VMEM((Q + 8, 256), f32),
            pltpu.VMEM((128, 512), f32),
            pltpu.VMEM((8, Q), f32),
        ],
        name="states",
        compiler_params=PARAMS,
    )(x_in, b_in, c_in, rim, run, late, conv_x, conv_bc)


def inside_kernel(skip_ref, xc_ref, bc_ref, run_ref, step_ref, y_ref):
    b = bc_ref[:, :128]
    c = bc_ref[:, 128:]
    run = run_ref[...]
    dt = step_ref[...]
    run_t = jnp.transpose(run)
    row = lax.broadcasted_iota(jnp.int32, (Q, Q), 0)
    col = lax.broadcasted_iota(jnp.int32, (Q, Q), 1)
    scores = jnp.where(row >= col, dot_t(c, b), 0.0)
    low = col < 64
    for p in range(4):
        h = 2 * p
        cols = slice(128 * p, 128 * p + 128)
        xf = xc_ref[:, cols].astype(f32)
        xb = jnp.concatenate(
            [jnp.where(low, xf, 0.0).astype(bf16), jnp.where(low, 0.0, xf).astype(bf16)], axis=0
        )
        mix = []
        for k in (h, h + 1):
            fade = jnp.exp(jnp.minimum(run_t[:, k : k + 1] - run[k : k + 1, :], 0.0))
            mix.append((fade * scores * dt[k : k + 1, :]).astype(bf16))
        skip = jnp.where(low[:1], skip_ref[h], skip_ref[h + 1])
        y_ref[:, cols] = dot(jnp.concatenate(mix, axis=1), xb) + skip * xf


def inside(xc, bc, run, step, d_skip):
    rows = lambda n: pl.BlockSpec((Q, n), lambda i: (i, 0))
    lanes = pl.BlockSpec((8, Q), lambda i: (0, i))
    return pl.pallas_call(
        inside_kernel,
        grid=(1024 // Q,),
        in_specs=[
            pl.BlockSpec(memory_space=pltpu.SMEM), rows(512), rows(256), lanes, lanes,
        ],
        out_specs=rows(512),
        out_shape=jax.ShapeDtypeStruct((1024, 512), f32),
        name="inside",
        compiler_params=PARAMS,
    )(d_skip, in_hbm(xc), bc, run, step)


def prefix_kernel(in_ref, out_ref):
    acc = jnp.zeros((32, 128), f32)
    for j in range(16):
        out_ref[j] = acc.astype(bf16)
        if j < 15:
            t = in_ref[j, 32:40, :].astype(f32)
            decay = jnp.exp(t[0:1] + t[1:2])
            acc = acc * decay + in_ref[j, 0:32, :].astype(f32)


def prefix(msg):
    return pl.pallas_call(
        prefix_kernel, out_shape=jax.ShapeDtypeStruct((16, 32, 128), bf16), name="prefix",
        compiler_params=PARAMS
    )(msg)


SETS = ((0, 1, 0), (0, 3, 1), (1, 1, 2), (1, 3, 3))
WIDTHS = (1152, 1024, 1024, 1024)


def projected(g_ref, w_ref, q, out, here, axis, picks):
    parts = []
    for pick in picks:
        for k in range(4):
            mask = pick * 4 + k if axis == 0 else k * 4 + pick
            owner = jnp.bitwise_xor(here, mask)
            parts.append(g_ref[pl.ds(pl.multiple_of(owner * 64, 64), 64), :])
    rows = jnp.concatenate(parts, axis=0)
    out[:, :1024] = dot(rows[:, :512], w_ref[:, q * 1024 : q * 1024 + 1024]).astype(bf16)
    if out.shape[1] > 1024:
        out[:, 1024:] = rows[:, 512:]


def gate_kernel(
    y_ref, bc_ref, grow_ref, before_ref, states_hbm, z_hbm, sin_ref, gain_ref, w_ref,
    *rest,
):
    outs, (st, g, w, zs, ss, b0, b1, b2, b3, sems) = rest[:9], rest[9:]
    i = pl.program_id(0)
    here = lax.axis_index("head")
    bufs = (b0, b1, b2, b3)

    def out_copy(n):
        if n == 8:
            return pltpu.make_async_copy(g, outs[8], sems.at[8])
        q, part = n % 4, n // 4
        return pltpu.make_async_copy(
            bufs[q].at[part * 256 : part * 256 + 256], outs[n], sems.at[n]
        )

    def w_copy(q):
        cols = slice(1024 * q, 1024 * q + 1024)
        return pltpu.make_async_copy(w_ref.at[:, cols], w.at[:, cols], sems.at[9 + q])

    def in_copies(k):
        part = pl.ds(pl.multiple_of(k * Q, Q), Q)
        return (
            pltpu.make_async_copy(z_hbm.at[part, :], zs.at[part, :], sems.at[13 + k]),
            pltpu.make_async_copy(states_hbm.at[part, :], ss.at[part, :], sems.at[21 + k]),
        )

    @pl.when(i == 0)
    def _():
        for k in range(8):
            for copy in in_copies(k):
                copy.start()
        for q in range(4):
            w_copy(q).start()
        for j in range(16):
            group, p = j // 4, j % 4
            st[32 * group : 32 * group + 32, 128 * p : 128 * p + 128] = sin_ref[j].astype(f32)

    @pl.when(i < 8)
    def _():
        for copy in in_copies(i):
            copy.wait()
        before = jnp.exp(before_ref[...])
        low1 = lax.broadcasted_iota(jnp.int32, (1, 128), 1) < 64
        grow = dot(grow_ref[...], spread())
        c = bc_ref[:, 128:]
        squares = jnp.zeros((Q, 128), f32)
        rows = pl.ds(pl.multiple_of(i * Q, Q), Q)
        for p in range(4):
            cols = slice(128 * p, 128 * p + 128)
            entering = ss[rows, cols].astype(f32) + st[:, cols] * pair_row(
                low1, before, 2 * p
            )
            ssd = y_ref[:, cols] + grow[:, cols] * dot(c, entering.astype(bf16))
            v = ssd * silu(zs[rows, cols].astype(f32))
            squares = squares + v * v
            g[rows, cols] = (v * gain_ref[:, cols]).astype(bf16)
        g[rows, 512:] = dot(squares.astype(bf16), jnp.ones((128, 128), bf16)).astype(bf16)

    for q, (ax, m, _) in enumerate(SETS):

        @pl.when(i == 8 + q)
        def _(q=q, ax=ax, m=m):
            w_copy(q).wait()
            projected(g, w, q, bufs[q], here, ax, (2, m))
            out_copy(q).start()
            out_copy(4 + q).start()

    @pl.when(i == 8)
    def _():
        out_copy(8).start()

    @pl.when(i == 11)
    def _():
        for n in range(9):
            out_copy(n).wait()


def gate(y, bc, grow, before, states, z_gate, incoming, gain, w_out):
    row = lambda i: jnp.minimum(i, 7)
    rows = lambda n: pl.BlockSpec((Q, n), lambda i: (row(i), 0))
    full = lambda *s: pl.BlockSpec(s, lambda i: (0,) * len(s))
    lanes = pl.BlockSpec((8, Q), lambda i: (0, row(i)))
    anywhere = pl.BlockSpec(memory_space=pl.ANY)
    return pl.pallas_call(
        gate_kernel,
        grid=(12,),
        in_specs=[
            rows(512), rows(256), rows(16), lanes, anywhere, anywhere, full(16, 32, 128),
            full(1, 512), anywhere,
        ],
        out_specs=[pl.BlockSpec(memory_space=pl.ANY)] * 9,
        out_shape=[jax.ShapeDtypeStruct((256, n), bf16) for n in WIDTHS * 2]
        + [jax.ShapeDtypeStruct((1024, 640), bf16)],
        scratch_shapes=[
            pltpu.VMEM((128, 512), f32),
            pltpu.VMEM((1024, 640), bf16),
            pltpu.VMEM((512, 4096), bf16),
            pltpu.VMEM((1024, 512), bf16),
            pltpu.VMEM((1024, 512), bf16),
        ]
        + [pltpu.VMEM((512, n), bf16) for n in WIDTHS]
        + [pltpu.SemaphoreType.DMA((29,))],
        name="gate",
        compiler_params=PARAMS,
    )(y, bc, grow, before, in_hbm(states), in_hbm(z_gate), incoming, gain, in_hbm(w_out))


def keep_kernel(g_ref, w_ref, *rest):
    outs, (b0, b1, b2, b3, sems) = rest[:8], rest[8:]
    bufs = (b0, b1, b2, b3)
    i = pl.program_id(0)
    here = lax.axis_index("head")

    def out_copy(n):
        q, part = n % 4, n // 4
        return pltpu.make_async_copy(
            bufs[q].at[part * 256 : part * 256 + 256], outs[n], sems.at[n]
        )

    for q, (ax, m, _) in enumerate(SETS):

        @pl.when(i == q)
        def _(q=q, ax=ax, m=m):
            projected(g_ref, w_ref, q, bufs[q], here, ax, (m ^ 2, 0))
            out_copy(q).start()
            out_copy(4 + q).start()

    @pl.when(i == 3)
    def _():
        for n in range(8):
            out_copy(n).wait()


def keep(g, w_out):
    return pl.pallas_call(
        keep_kernel,
        grid=(4,),
        in_specs=[
            pl.BlockSpec((1024, 640), lambda i: (0, 0)),
            pl.BlockSpec(memory_space=pltpu.VMEM),
        ],
        out_specs=[pl.BlockSpec(memory_space=pl.ANY)] * 8,
        out_shape=[jax.ShapeDtypeStruct((256, n), bf16) for n in WIDTHS * 2],
        scratch_shapes=[pltpu.VMEM((512, n), bf16) for n in WIDTHS]
        + [pltpu.SemaphoreType.DMA((8,))],
        name="keep",
        compiler_params=PARAMS,
    )(g, pltpu.with_memory_space_constraint(w_out, pltpu.VMEM))


def swap(values, axis, mask):
    mask = mask * 4 if axis == 0 else mask
    return lax.ppermute(values, "head", [(h, h ^ mask) for h in range(16)])


def added(*values):
    total = values[0].astype(f32)
    for v in values[1:]:
        total = total + v.astype(f32)
    return total


def summed_to_owners(g, sends, w_out):
    far = []
    for q, (ax, m, _) in enumerate(SETS):
        far.append(swap(sends[q], ax, m))
    near = []
    for q, (ax, m, _) in enumerate(SETS):
        near.append(swap(sends[4 + q], ax, m))
    kept = keep(g, w_out)
    passed, own = kept[:4], kept[4:]
    second = [
        swap(added(a, b).astype(bf16), ax, m ^ 2) for a, b, (ax, m, q) in zip(passed, far, SETS)
    ]
    later = []
    for (ax, m, q), a, b, c in zip(SETS, own, near, second):
        total = added(a, b, c).reshape(4, 64, -1)
        away = jnp.stack([total[m], total[2]]).astype(bf16)
        later.append((total[0], total[m ^ 2], swap(away, 1 - ax, m)))
    last = []
    for (ax, m, q), (first, second, got) in zip(SETS, later):
        last.append(
            (
                added(first, got[0]),
                swap(added(second, got[1]).astype(bf16), 1 - ax, m ^ 2),
            )
        )
    parts = [added(a, b) for a, b in last]
    scale = lax.rsqrt(parts[0][:, 1024:1025] / INNER + norm_eps)
    return jnp.concatenate([v[:, :1024] * scale for v in parts], axis=1).astype(bf16)


def layer(x_in, z_gate, b_in, c_in, dt_raw, a_log, d_skip, conv_x, conv_bc, norm_gain, w_out):
    rim = lax.ppermute(
        edge_rows(x_in, b_in, c_in), "seq", [(i, i + 1) for i in range(15)]
    )
    run, step, late, grow = decays(dt_raw, a_log)
    xc, bc, before, states, msg = block_states(
        x_in, b_in, c_in, rim, run, late, conv_x, conv_bc
    )
    pieces = prefix(lax.all_to_all(msg, "seq", 0, 0))
    incoming = lax.all_to_all(pieces, "seq", 0, 0)
    y = inside(xc, bc, run, step, d_skip)
    *sends, g = gate(
        y, bc, grow, before, states, z_gate, incoming, norm_gain[None, :], w_out
    )
    return summed_to_owners(g, sends, w_out)


def solution(mesh):
    in_specs = (
        P("seq", "head"),
        P("seq", "head"),
        P("seq", None),
        P("seq", None),
        P("seq", "head"),
        P("head"),
        P("head"),
        P(None, "head"),
        P(),
        P("head"),
        P("head", None),
    )
    out_specs = P(("seq", "head"), None)
    return jax.shard_map(layer, mesh=mesh, in_specs=in_specs, out_specs=out_specs, check_vma=False)
```

```python
import jax
import jax.numpy as jnp
from jax import lax
from jax.experimental import pallas as pl
from jax.experimental.pallas import tpu as pltpu
from jax.sharding import PartitionSpec as P


INNER = 8192
norm_eps = 1e-05
Q = 128
PARAMS = pltpu.CompilerParams(vmem_limit_bytes=24 * 2**20)
bf16 = jnp.bfloat16
f32 = jnp.float32


def in_hbm(v):
    return pltpu.with_memory_space_constraint(v, pltpu.HBM)


def silu(v):
    half = 0.5 * v
    return half + half * jnp.tanh(half)


def dot(a, b):
    return jnp.dot(a, b, preferred_element_type=f32)


def dot_t(a, b):
    return lax.dot_general(a, b, (((1,), (1,)), ((), ())), preferred_element_type=f32)


def head_column(ref, shape):
    rows = lax.broadcasted_iota(jnp.int32, shape, 0)
    out = jnp.full(shape, ref[0], f32)
    for h in range(1, 8):
        out = jnp.where(rows == h, ref[h], out)
    return out


def edge_kernel(x_ref, b_ref, c_ref, o_ref):
    o_ref[:, :512] = x_ref[...]
    o_ref[:, 512:640] = b_ref[...]
    o_ref[:, 640:] = c_ref[...]


def edge_rows(x_in, b_in, c_in):
    last = lambda n: pl.BlockSpec((16, n), lambda i: (63, 0))
    return pl.pallas_call(
        edge_kernel,
        grid=(1,),
        in_specs=[last(512), last(128), last(128)],
        out_specs=pl.BlockSpec((16, 768), lambda i: (0, 0)),
        out_shape=jax.ShapeDtypeStruct((16, 768), bf16),
        name="edge",
        compiler_params=PARAMS,
    )(in_hbm(x_in), in_hbm(b_in), in_hbm(c_in))


def pair_row(low, values, h):
    return jnp.where(low, values[h : h + 1, :], values[h + 1 : h + 2, :])


def decay_kernel(a_ref, dt_ref, run_ref, step_ref, late_ref, grow_ref):
    rate = -jnp.exp(head_column(a_ref, (8, Q)))
    lane8 = lax.broadcasted_iota(jnp.int32, (8, Q), 1)

    def halves(v):
        high = v.astype(bf16).astype(f32)
        return jnp.transpose(jnp.concatenate([high, v - high], axis=0)).astype(bf16)

    for i in range(1024 // Q):
        lanes = slice(i * Q, i * Q + Q)
        raw = dt_ref[:, lanes]
        dt = jnp.maximum(raw, 0.0) + jnp.log1p(jnp.exp(-jnp.abs(raw)))
        run = rate * dt
        shift = 1
        while shift < Q:
            run = run + jnp.where(lane8 >= shift, pltpu.roll(run, shift, 1), 0.0)
            shift *= 2
        fin = jnp.broadcast_to(run[:, Q - 1 : Q], (8, Q))
        run_ref[:, lanes] = run
        step_ref[:, lanes] = dt
        late_ref[lanes, :] = halves(jnp.exp(jnp.minimum(fin - run, 0.0)) * dt)
        grow_ref[lanes, :] = halves(jnp.exp(run))


def decays(dt_raw, a_log):
    full = lambda *s: pl.BlockSpec(s, lambda i: (0,) * len(s))
    return pl.pallas_call(
        decay_kernel,
        grid=(1,),
        in_specs=[pl.BlockSpec(memory_space=pltpu.SMEM), full(8, 1024)],
        out_specs=[full(8, 1024)] * 2 + [full(1024, 16)] * 2,
        out_shape=[jax.ShapeDtypeStruct((8, 1024), f32)] * 2
        + [jax.ShapeDtypeStruct((1024, 16), bf16)] * 2,
        name="decays",
        compiler_params=PARAMS,
    )(a_log, dt_raw.T)


def spread():
    lane = lax.broadcasted_iota(jnp.int32, (16, 512), 1)
    row = lax.broadcasted_iota(jnp.int32, (16, 512), 0)
    first = jnp.where(row >= 8, row - 8, row) * 64
    return jnp.where((lane >= first) & (lane < first + 64), 1.0, 0.0).astype(bf16)


def state_kernel(
    x_ref, b_ref, c_ref, rim_ref, run_ref, late_ref, wx_ref, wbc_ref,
    xc_hbm, bc_ref, before_ref, states_hbm, msg_ref,
    xs, bs, st, tot, xc_ref, states_ref, sems,
):
    i = pl.program_id(0)
    here = pl.ds(pl.multiple_of(i * Q, Q), Q)

    def out_copies(k):
        part = pl.ds(pl.multiple_of(k * Q, Q), Q)
        return (
            pltpu.make_async_copy(xc_ref.at[part, :], xc_hbm.at[part, :], sems.at[k]),
            pltpu.make_async_copy(states_ref.at[part, :], states_hbm.at[part, :], sems.at[8 + k]),
        )

    @pl.when(i == 0)
    def _():
        xs[0:8, :] = rim_ref[8:16, :512].astype(f32)
        bs[0:8, :] = rim_ref[8:16, 512:].astype(f32)
        st[...] = jnp.zeros_like(st)
        tot[...] = jnp.zeros_like(tot)

    @pl.when(i > 0)
    def _():
        xs[0:8, :] = xs[Q : Q + 8, :]
        bs[0:8, :] = bs[Q : Q + 8, :]

    xs[8 : Q + 8, :] = x_ref[...].astype(f32)
    bs[8 : Q + 8, :128] = b_ref[...].astype(f32)
    bs[8 : Q + 8, 128:] = c_ref[...].astype(f32)

    def conv(buf, w_ref, cols):
        whole = buf[:, cols]
        half = 0.5 * w_ref[:, cols]
        total = half[3:4] * whole[8:]
        for k in range(3):
            total = total + half[k : k + 1] * pltpu.roll(whole, 3 - k, 0)[8:]
        return total + total * jnp.tanh(total)

    fin = jnp.broadcast_to(run_ref[:, Q - 1 : Q], (8, 128))
    b = conv(bs, wbc_ref, slice(0, 128))
    bc_ref[:, :128] = b.astype(bf16)
    bc_ref[:, 128:] = conv(bs, wbc_ref, slice(128, 256)).astype(bf16)
    b_t = jnp.transpose(b).astype(bf16)
    low1 = lax.broadcasted_iota(jnp.int32, (1, 128), 1) < 64
    late = dot(late_ref[...], spread())
    states_ref[here, :] = st[...].astype(bf16)
    before_ref[...] = tot[...]
    for p in range(4):
        cols = slice(128 * p, 128 * p + 128)
        xp = conv(xs, wx_ref, cols)
        xc_ref[here, cols] = xp.astype(bf16)
        end = jnp.exp(pair_row(low1, fin, 2 * p))
        st[:, cols] = st[:, cols] * end + dot(b_t, (xp * late[:, cols]).astype(bf16))
    tot[...] = tot[...] + fin
    for copy in out_copies(i):
        copy.start()

    @pl.when(i == pl.num_programs(0) - 1)
    def _():
        total = tot[...]
        row8 = lax.broadcasted_iota(jnp.int32, (8, 128), 0)
        for p in range(4):
            decay = jnp.broadcast_to(pair_row(low1, total, 2 * p), (8, 128))
            high = decay.astype(bf16).astype(f32)
            tile = jnp.where(row8 == 0, high, decay - high).astype(bf16)
            for group in range(4):
                j = 4 * group + p
                msg_ref[j, 0:32, :] = st[
                    32 * group : 32 * group + 32, 128 * p : 128 * p + 128
                ].astype(bf16)
                msg_ref[j, 32:40, :] = tile
        for k in range(8):
            for copy in out_copies(k):
                copy.wait()


def block_states(x_in, b_in, c_in, rim, run, late, conv_x, conv_bc):
    rows = lambda n: pl.BlockSpec((Q, n), lambda i: (i, 0))
    full = lambda *s: pl.BlockSpec(s, lambda i: (0,) * len(s))
    lanes = pl.BlockSpec((8, Q), lambda i: (0, i))
    anywhere = pl.BlockSpec(memory_space=pl.ANY)
    return pl.pallas_call(
        state_kernel,
        grid=(1024 // Q,),
        in_specs=[
            rows(512), rows(128), rows(128), full(16, 768), lanes, rows(16),
            full(4, 512), full(4, 256),
        ],
        out_specs=[anywhere, rows(256), lanes, anywhere, full(16, 40, 128)],
        out_shape=[
            pltpu.HBM((1024, 512), bf16),
            jax.ShapeDtypeStruct((1024, 256), bf16),
            jax.ShapeDtypeStruct((8, 1024), f32),
            pltpu.HBM((1024, 512), bf16),
            jax.ShapeDtypeStruct((16, 40, 128), bf16),
        ],
        scratch_shapes=[
            pltpu.VMEM((Q + 8, 512), f32),
            pltpu.VMEM((Q + 8, 256), f32),
            pltpu.VMEM((128, 512), f32),
            pltpu.VMEM((8, Q), f32),
            pltpu.VMEM((1024, 512), bf16),
            pltpu.VMEM((1024, 512), bf16),
            pltpu.SemaphoreType.DMA((16,)),
        ],
        name="states",
        compiler_params=PARAMS,
    )(x_in, b_in, c_in, rim, run, late, conv_x, conv_bc)


def inside_kernel(skip_ref, xc_ref, bc_ref, run_ref, step_ref, y_ref):
    b = bc_ref[:, :128]
    c = bc_ref[:, 128:]
    run = run_ref[...]
    dt = step_ref[...]
    run_t = jnp.transpose(run)
    row = lax.broadcasted_iota(jnp.int32, (Q, Q), 0)
    col = lax.broadcasted_iota(jnp.int32, (Q, Q), 1)
    scores = jnp.where(row >= col, dot_t(c, b), 0.0)
    low = col < 64
    for p in range(4):
        h = 2 * p
        cols = slice(128 * p, 128 * p + 128)
        xf = xc_ref[:, cols].astype(f32)
        xb = jnp.concatenate(
            [jnp.where(low, xf, 0.0).astype(bf16), jnp.where(low, 0.0, xf).astype(bf16)], axis=0
        )
        mix = []
        for k in (h, h + 1):
            fade = jnp.exp(jnp.minimum(run_t[:, k : k + 1] - run[k : k + 1, :], 0.0))
            mix.append((fade * scores * dt[k : k + 1, :]).astype(bf16))
        skip = jnp.where(low[:1], skip_ref[h], skip_ref[h + 1])
        y_ref[:, cols] = dot(jnp.concatenate(mix, axis=1), xb) + skip * xf


def inside(xc, bc, run, step, d_skip):
    rows = lambda n: pl.BlockSpec((Q, n), lambda i: (i, 0))
    lanes = pl.BlockSpec((8, Q), lambda i: (0, i))
    return pl.pallas_call(
        inside_kernel,
        grid=(1024 // Q,),
        in_specs=[
            pl.BlockSpec(memory_space=pltpu.SMEM), rows(512), rows(256), lanes, lanes,
        ],
        out_specs=rows(512),
        out_shape=jax.ShapeDtypeStruct((1024, 512), f32),
        name="inside",
        compiler_params=PARAMS,
    )(d_skip, in_hbm(xc), bc, run, step)


def prefix_kernel(in_ref, out_ref):
    acc = jnp.zeros((32, 128), f32)
    for j in range(16):
        out_ref[j] = acc.astype(bf16)
        if j < 15:
            t = in_ref[j, 32:40, :].astype(f32)
            decay = jnp.exp(t[0:1] + t[1:2])
            acc = acc * decay + in_ref[j, 0:32, :].astype(f32)


def prefix(msg):
    return pl.pallas_call(
        prefix_kernel, out_shape=jax.ShapeDtypeStruct((16, 32, 128), bf16), name="prefix",
        compiler_params=PARAMS
    )(msg)


SETS = ((0, 1, 0), (0, 3, 1), (1, 1, 2), (1, 3, 3))
WIDTHS = (1152, 1024, 1024, 1024)


def projected(g_ref, w_ref, q, out, here, axis, picks):
    parts = []
    for pick in picks:
        for k in range(4):
            mask = pick * 4 + k if axis == 0 else k * 4 + pick
            owner = jnp.bitwise_xor(here, mask)
            parts.append(g_ref[pl.ds(pl.multiple_of(owner * 64, 64), 64), :])
    rows = jnp.concatenate(parts, axis=0)
    out[:, :1024] = dot(rows[:, :512], w_ref[:, q * 1024 : q * 1024 + 1024]).astype(bf16)
    if out.shape[1] > 1024:
        out[:, 1024:] = rows[:, 512:]


def gate_kernel(
    y_ref, bc_ref, grow_ref, before_ref, states_hbm, z_hbm, sin_ref, gain_ref, w_ref,
    *rest,
):
    outs, (st, g, w, zs, ss, b0, b1, b2, b3, sems) = rest[:9], rest[9:]
    i = pl.program_id(0)
    here = lax.axis_index("head")
    bufs = (b0, b1, b2, b3)

    def out_copy(n):
        if n == 8:
            return pltpu.make_async_copy(g, outs[8], sems.at[8])
        q, part = n % 4, n // 4
        return pltpu.make_async_copy(
            bufs[q].at[part * 256 : part * 256 + 256], outs[n], sems.at[n]
        )

    def w_copy(q):
        cols = slice(1024 * q, 1024 * q + 1024)
        return pltpu.make_async_copy(w_ref.at[:, cols], w.at[:, cols], sems.at[9 + q])

    def in_copies(k):
        part = pl.ds(pl.multiple_of(k * Q, Q), Q)
        return (
            pltpu.make_async_copy(z_hbm.at[part, :], zs.at[part, :], sems.at[13 + k]),
            pltpu.make_async_copy(states_hbm.at[part, :], ss.at[part, :], sems.at[21 + k]),
        )

    @pl.when(i == 0)
    def _():
        for k in range(8):
            for copy in in_copies(k):
                copy.start()
        for q in range(4):
            w_copy(q).start()
        for j in range(16):
            group, p = j // 4, j % 4
            st[32 * group : 32 * group + 32, 128 * p : 128 * p + 128] = sin_ref[j].astype(f32)

    @pl.when(i < 8)
    def _():
        for copy in in_copies(i):
            copy.wait()
        before = jnp.exp(before_ref[...])
        low1 = lax.broadcasted_iota(jnp.int32, (1, 128), 1) < 64
        grow = dot(grow_ref[...], spread())
        c = bc_ref[:, 128:]
        squares = jnp.zeros((Q, 128), f32)
        rows = pl.ds(pl.multiple_of(i * Q, Q), Q)
        for p in range(4):
            cols = slice(128 * p, 128 * p + 128)
            entering = ss[rows, cols].astype(f32) + st[:, cols] * pair_row(
                low1, before, 2 * p
            )
            ssd = y_ref[rows, cols] + grow[:, cols] * dot(c, entering.astype(bf16))
            v = ssd * silu(zs[rows, cols].astype(f32))
            squares = squares + v * v
            g[rows, cols] = (v * gain_ref[:, cols]).astype(bf16)
        g[rows, 512:] = dot(squares.astype(bf16), jnp.ones((128, 128), bf16)).astype(bf16)

    for q, (ax, m, _) in enumerate(SETS):

        @pl.when(i == 8 + q)
        def _(q=q, ax=ax, m=m):
            w_copy(q).wait()
            projected(g, w, q, bufs[q], here, ax, (2, m))
            out_copy(q).start()
            out_copy(4 + q).start()

    @pl.when(i == 8)
    def _():
        out_copy(8).start()

    @pl.when(i == 11)
    def _():
        for n in range(9):
            out_copy(n).wait()


def gate(y, bc, grow, before, states, z_gate, incoming, gain, w_out):
    row = lambda i: jnp.minimum(i, 7)
    rows = lambda n: pl.BlockSpec((Q, n), lambda i: (row(i), 0))
    full = lambda *s: pl.BlockSpec(s, lambda i: (0,) * len(s))
    lanes = pl.BlockSpec((8, Q), lambda i: (0, row(i)))
    anywhere = pl.BlockSpec(memory_space=pl.ANY)
    return pl.pallas_call(
        gate_kernel,
        grid=(12,),
        in_specs=[
            pl.BlockSpec(memory_space=pltpu.VMEM), rows(256), rows(16), lanes, anywhere, anywhere,
            full(16, 32, 128),
            full(1, 512), anywhere,
        ],
        out_specs=[pl.BlockSpec(memory_space=pl.ANY)] * 9,
        out_shape=[jax.ShapeDtypeStruct((256, n), bf16) for n in WIDTHS * 2]
        + [jax.ShapeDtypeStruct((1024, 640), bf16)],
        scratch_shapes=[
            pltpu.VMEM((128, 512), f32),
            pltpu.VMEM((1024, 640), bf16),
            pltpu.VMEM((512, 4096), bf16),
            pltpu.VMEM((1024, 512), bf16),
            pltpu.VMEM((1024, 512), bf16),
        ]
        + [pltpu.VMEM((512, n), bf16) for n in WIDTHS]
        + [pltpu.SemaphoreType.DMA((29,))],
        name="gate",
        compiler_params=PARAMS,
    )(y, bc, grow, before, in_hbm(states), in_hbm(z_gate), incoming, gain, in_hbm(w_out))


def keep_kernel(g_ref, w_ref, *rest):
    outs, (b0, b1, b2, b3, sems) = rest[:8], rest[8:]
    bufs = (b0, b1, b2, b3)
    i = pl.program_id(0)
    here = lax.axis_index("head")

    def out_copy(n):
        q, part = n % 4, n // 4
        return pltpu.make_async_copy(
            bufs[q].at[part * 256 : part * 256 + 256], outs[n], sems.at[n]
        )

    for q, (ax, m, _) in enumerate(SETS):

        @pl.when(i == q)
        def _(q=q, ax=ax, m=m):
            projected(g_ref, w_ref, q, bufs[q], here, ax, (m ^ 2, 0))
            out_copy(q).start()
            out_copy(4 + q).start()

    @pl.when(i == 3)
    def _():
        for n in range(8):
            out_copy(n).wait()


def keep(g, w_out):
    return pl.pallas_call(
        keep_kernel,
        grid=(4,),
        in_specs=[
            pl.BlockSpec((1024, 640), lambda i: (0, 0)),
            pl.BlockSpec(memory_space=pltpu.VMEM),
        ],
        out_specs=[pl.BlockSpec(memory_space=pl.ANY)] * 8,
        out_shape=[jax.ShapeDtypeStruct((256, n), bf16) for n in WIDTHS * 2],
        scratch_shapes=[pltpu.VMEM((512, n), bf16) for n in WIDTHS]
        + [pltpu.SemaphoreType.DMA((8,))],
        name="keep",
        compiler_params=PARAMS,
    )(g, pltpu.with_memory_space_constraint(w_out, pltpu.VMEM))


def swap(values, axis, mask):
    mask = mask * 4 if axis == 0 else mask
    return lax.ppermute(values, "head", [(h, h ^ mask) for h in range(16)])


def added(*values):
    total = values[0].astype(f32)
    for v in values[1:]:
        total = total + v.astype(f32)
    return total


def summed_to_owners(g, sends, w_out):
    far = []
    for q, (ax, m, _) in enumerate(SETS):
        far.append(swap(sends[q], ax, m))
    near = []
    for q, (ax, m, _) in enumerate(SETS):
        near.append(swap(sends[4 + q], ax, m))
    kept = keep(g, w_out)
    passed, own = kept[:4], kept[4:]
    second = [
        swap(added(a, b).astype(bf16), ax, m ^ 2) for a, b, (ax, m, q) in zip(passed, far, SETS)
    ]
    later = []
    for (ax, m, q), a, b, c in zip(SETS, own, near, second):
        total = added(a, b, c).reshape(4, 64, -1)
        away = jnp.stack([total[m], total[2]]).astype(bf16)
        later.append((total[0], total[m ^ 2], swap(away, 1 - ax, m)))
    last = []
    for (ax, m, q), (first, second, got) in zip(SETS, later):
        last.append(
            (
                added(first, got[0]),
                swap(added(second, got[1]).astype(bf16), 1 - ax, m ^ 2),
            )
        )
    parts = [added(a, b) for a, b in last]
    scale = lax.rsqrt(parts[0][:, 1024:1025] / INNER + norm_eps)
    return jnp.concatenate([v[:, :1024] * scale for v in parts], axis=1).astype(bf16)


def layer(x_in, z_gate, b_in, c_in, dt_raw, a_log, d_skip, conv_x, conv_bc, norm_gain, w_out):
    rim = lax.ppermute(
        edge_rows(x_in, b_in, c_in), "seq", [(i, i + 1) for i in range(15)]
    )
    run, step, late, grow = decays(dt_raw, a_log)
    xc, bc, before, states, msg = block_states(
        x_in, b_in, c_in, rim, run, late, conv_x, conv_bc
    )
    pieces = prefix(lax.all_to_all(msg, "seq", 0, 0))
    incoming = lax.all_to_all(pieces, "seq", 0, 0)
    y = inside(xc, bc, run, step, d_skip)
    *sends, g = gate(
        y, bc, grow, before, states, z_gate, incoming, norm_gain[None, :], w_out
    )
    return summed_to_owners(g, sends, w_out)


def solution(mesh):
    in_specs = (
        P("seq", "head"),
        P("seq", "head"),
        P("seq", None),
        P("seq", None),
        P("seq", "head"),
        P("head"),
        P("head"),
        P(None, "head"),
        P(),
        P("head"),
        P("head", None),
    )
    out_specs = P(("seq", "head"), None)
    return jax.shard_map(layer, mesh=mesh, in_specs=in_specs, out_specs=out_specs, check_vma=False)
```

```python
import functools

import jax
import jax.numpy as jnp
from jax import lax
from jax.experimental import pallas as pl
from jax.experimental.pallas import tpu as pltpu
from jax.sharding import PartitionSpec as P


INNER = 8192
norm_eps = 1e-05
Q = 128
PARAMS = pltpu.CompilerParams(vmem_limit_bytes=24 * 2**20)
bf16 = jnp.bfloat16
f32 = jnp.float32


def in_hbm(v):
    return pltpu.with_memory_space_constraint(v, pltpu.HBM)


def silu(v):
    half = 0.5 * v
    return half + half * jnp.tanh(half)


def dot(a, b):
    return jnp.dot(a, b, preferred_element_type=f32)


def dot_t(a, b):
    return lax.dot_general(a, b, (((1,), (1,)), ((), ())), preferred_element_type=f32)


def head_column(ref, shape):
    rows = lax.broadcasted_iota(jnp.int32, shape, 0)
    out = jnp.full(shape, ref[0], f32)
    for h in range(1, 8):
        out = jnp.where(rows == h, ref[h], out)
    return out


def edge_kernel(x_ref, b_ref, c_ref, o_ref):
    o_ref[:, :512] = x_ref[...]
    o_ref[:, 512:640] = b_ref[...]
    o_ref[:, 640:] = c_ref[...]


def edge_rows(x_in, b_in, c_in):
    last = lambda n: pl.BlockSpec((16, n), lambda i: (63, 0))
    return pl.pallas_call(
        edge_kernel,
        grid=(1,),
        in_specs=[last(512), last(128), last(128)],
        out_specs=pl.BlockSpec((16, 768), lambda i: (0, 0)),
        out_shape=jax.ShapeDtypeStruct((16, 768), bf16),
        name="edge",
        compiler_params=PARAMS,
    )(in_hbm(x_in), in_hbm(b_in), in_hbm(c_in))


def pair_row(low, values, h):
    return jnp.where(low, values[h : h + 1, :], values[h + 1 : h + 2, :])


def decay_kernel(a_ref, dt_ref, run_ref, step_ref, late_ref, grow_ref):
    rate = -jnp.exp(head_column(a_ref, (8, Q)))
    lane8 = lax.broadcasted_iota(jnp.int32, (8, Q), 1)

    def halves(v):
        high = v.astype(bf16).astype(f32)
        return jnp.transpose(jnp.concatenate([high, v - high], axis=0)).astype(bf16)

    for i in range(1024 // Q):
        lanes = slice(i * Q, i * Q + Q)
        raw = dt_ref[:, lanes]
        dt = jnp.maximum(raw, 0.0) + jnp.log1p(jnp.exp(-jnp.abs(raw)))
        run = rate * dt
        shift = 1
        while shift < Q:
            run = run + jnp.where(lane8 >= shift, pltpu.roll(run, shift, 1), 0.0)
            shift *= 2
        fin = jnp.broadcast_to(run[:, Q - 1 : Q], (8, Q))
        run_ref[:, lanes] = run
        step_ref[:, lanes] = dt
        late_ref[lanes, :] = halves(jnp.exp(jnp.minimum(fin - run, 0.0)) * dt)
        grow_ref[lanes, :] = halves(jnp.exp(run))


def decays(dt_raw, a_log):
    full = lambda *s: pl.BlockSpec(s, lambda i: (0,) * len(s))
    return pl.pallas_call(
        decay_kernel,
        grid=(1,),
        in_specs=[pl.BlockSpec(memory_space=pltpu.SMEM), full(8, 1024)],
        out_specs=[full(8, 1024)] * 2 + [full(1024, 16)] * 2,
        out_shape=[jax.ShapeDtypeStruct((8, 1024), f32)] * 2
        + [jax.ShapeDtypeStruct((1024, 16), bf16)] * 2,
        name="decays",
        compiler_params=PARAMS,
    )(a_log, dt_raw.T)


def spread():
    lane = lax.broadcasted_iota(jnp.int32, (16, 512), 1)
    row = lax.broadcasted_iota(jnp.int32, (16, 512), 0)
    first = jnp.where(row >= 8, row - 8, row) * 64
    return jnp.where((lane >= first) & (lane < first + 64), 1.0, 0.0).astype(bf16)


def state_kernel(
    x_ref, b_ref, c_ref, rim_ref, run_ref, late_ref, wx_ref, wbc_ref,
    xc_hbm, bc_ref, before_ref, states_hbm, msg_ref,
    xs, bs, st, tot, xc_ref, states_ref, sems,
):
    i = pl.program_id(0)
    here = pl.ds(pl.multiple_of(i * Q, Q), Q)

    def out_copies(k):
        part = pl.ds(pl.multiple_of(k * Q, Q), Q)
        return (
            pltpu.make_async_copy(xc_ref.at[part, :], xc_hbm.at[part, :], sems.at[k]),
            pltpu.make_async_copy(states_ref.at[part, :], states_hbm.at[part, :], sems.at[8 + k]),
        )

    @pl.when(i == 0)
    def _():
        xs[0:8, :] = rim_ref[8:16, :512].astype(f32)
        bs[0:8, :] = rim_ref[8:16, 512:].astype(f32)
        st[...] = jnp.zeros_like(st)
        tot[...] = jnp.zeros_like(tot)

    @pl.when(i > 0)
    def _():
        xs[0:8, :] = xs[Q : Q + 8, :]
        bs[0:8, :] = bs[Q : Q + 8, :]

    xs[8 : Q + 8, :] = x_ref[...].astype(f32)
    bs[8 : Q + 8, :128] = b_ref[...].astype(f32)
    bs[8 : Q + 8, 128:] = c_ref[...].astype(f32)

    def conv(buf, w_ref, cols):
        whole = buf[:, cols]
        half = 0.5 * w_ref[:, cols]
        total = half[3:4] * whole[8:]
        for k in range(3):
            total = total + half[k : k + 1] * pltpu.roll(whole, 3 - k, 0)[8:]
        return total + total * jnp.tanh(total)

    fin = jnp.broadcast_to(run_ref[:, Q - 1 : Q], (8, 128))
    b = conv(bs, wbc_ref, slice(0, 128))
    bc_ref[:, :128] = b.astype(bf16)
    bc_ref[:, 128:] = conv(bs, wbc_ref, slice(128, 256)).astype(bf16)
    b_t = jnp.transpose(b).astype(bf16)
    low1 = lax.broadcasted_iota(jnp.int32, (1, 128), 1) < 64
    late = dot(late_ref[...], spread())
    states_ref[here, :] = st[...].astype(bf16)
    before_ref[...] = tot[...]
    for p in range(4):
        cols = slice(128 * p, 128 * p + 128)
        xp = conv(xs, wx_ref, cols)
        xc_ref[here, cols] = xp.astype(bf16)
        end = jnp.exp(pair_row(low1, fin, 2 * p))
        st[:, cols] = st[:, cols] * end + dot(b_t, (xp * late[:, cols]).astype(bf16))
    tot[...] = tot[...] + fin
    for copy in out_copies(i):
        copy.start()

    @pl.when(i == pl.num_programs(0) - 1)
    def _():
        total = tot[...]
        row8 = lax.broadcasted_iota(jnp.int32, (8, 128), 0)
        for p in range(4):
            decay = jnp.broadcast_to(pair_row(low1, total, 2 * p), (8, 128))
            high = decay.astype(bf16).astype(f32)
            tile = jnp.where(row8 == 0, high, decay - high).astype(bf16)
            for group in range(4):
                j = 4 * group + p
                msg_ref[j, 0:32, :] = st[
                    32 * group : 32 * group + 32, 128 * p : 128 * p + 128
                ].astype(bf16)
                msg_ref[j, 32:40, :] = tile
        for k in range(8):
            for copy in out_copies(k):
                copy.wait()


def block_states(x_in, b_in, c_in, rim, run, late, conv_x, conv_bc):
    rows = lambda n: pl.BlockSpec((Q, n), lambda i: (i, 0))
    full = lambda *s: pl.BlockSpec(s, lambda i: (0,) * len(s))
    lanes = pl.BlockSpec((8, Q), lambda i: (0, i))
    anywhere = pl.BlockSpec(memory_space=pl.ANY)
    return pl.pallas_call(
        state_kernel,
        grid=(1024 // Q,),
        in_specs=[
            rows(512), rows(128), rows(128), full(16, 768), lanes, rows(16),
            full(4, 512), full(4, 256),
        ],
        out_specs=[anywhere, rows(256), lanes, anywhere, full(16, 40, 128)],
        out_shape=[
            pltpu.HBM((1024, 512), bf16),
            jax.ShapeDtypeStruct((1024, 256), bf16),
            jax.ShapeDtypeStruct((8, 1024), f32),
            pltpu.HBM((1024, 512), bf16),
            jax.ShapeDtypeStruct((16, 40, 128), bf16),
        ],
        scratch_shapes=[
            pltpu.VMEM((Q + 8, 512), f32),
            pltpu.VMEM((Q + 8, 256), f32),
            pltpu.VMEM((128, 512), f32),
            pltpu.VMEM((8, Q), f32),
            pltpu.VMEM((1024, 512), bf16),
            pltpu.VMEM((1024, 512), bf16),
            pltpu.SemaphoreType.DMA((16,)),
        ],
        name="states",
        compiler_params=PARAMS,
    )(x_in, b_in, c_in, rim, run, late, conv_x, conv_bc)


def inside_kernel(skip_ref, xc_ref, bc_ref, run_ref, step_ref, y_ref):
    b = bc_ref[:, :128]
    c = bc_ref[:, 128:]
    run = run_ref[...]
    dt = step_ref[...]
    run_t = jnp.transpose(run)
    row = lax.broadcasted_iota(jnp.int32, (Q, Q), 0)
    col = lax.broadcasted_iota(jnp.int32, (Q, Q), 1)
    scores = jnp.where(row >= col, dot_t(c, b), 0.0)
    low = col < 64
    for p in range(4):
        h = 2 * p
        cols = slice(128 * p, 128 * p + 128)
        xf = xc_ref[:, cols].astype(f32)
        xb = jnp.concatenate(
            [jnp.where(low, xf, 0.0).astype(bf16), jnp.where(low, 0.0, xf).astype(bf16)], axis=0
        )
        mix = []
        for k in (h, h + 1):
            fade = jnp.exp(jnp.minimum(run_t[:, k : k + 1] - run[k : k + 1, :], 0.0))
            mix.append((fade * scores * dt[k : k + 1, :]).astype(bf16))
        skip = jnp.where(low[:1], skip_ref[h], skip_ref[h + 1])
        y_ref[:, cols] = dot(jnp.concatenate(mix, axis=1), xb) + skip * xf


def inside(xc, bc, run, step, d_skip):
    rows = lambda n: pl.BlockSpec((Q, n), lambda i: (i, 0))
    lanes = pl.BlockSpec((8, Q), lambda i: (0, i))
    return pl.pallas_call(
        inside_kernel,
        grid=(1024 // Q,),
        in_specs=[
            pl.BlockSpec(memory_space=pltpu.SMEM), rows(512), rows(256), lanes, lanes,
        ],
        out_specs=rows(512),
        out_shape=jax.ShapeDtypeStruct((1024, 512), f32),
        name="inside",
        compiler_params=PARAMS,
    )(d_skip, in_hbm(xc), bc, run, step)


def prefix_kernel(in_ref, out_ref):
    acc = jnp.zeros((32, 128), f32)
    for j in range(16):
        out_ref[j] = acc.astype(bf16)
        if j < 15:
            t = in_ref[j, 32:40, :].astype(f32)
            decay = jnp.exp(t[0:1] + t[1:2])
            acc = acc * decay + in_ref[j, 0:32, :].astype(f32)


def prefix(msg):
    return pl.pallas_call(
        prefix_kernel, out_shape=jax.ShapeDtypeStruct((16, 32, 128), bf16), name="prefix",
        compiler_params=PARAMS
    )(msg)


SETS = ((0, 1, 0), (0, 3, 1), (1, 1, 2), (1, 3, 3))
WIDTHS = (1152, 1024, 1024, 1024)


FIRST = (8, 9, 10, 11, 2, 6, 14)
REST = (0, 1, 3, 4, 5, 7, 12, 13, 15)


def projected(g_ref, w_ref, q, out, axis, picks, place=None):
    parts = []
    for pick in picks:
        for k in range(4):
            mask = pick * 4 + k if axis == 0 else k * 4 + pick
            at = 64 * (mask if place is None else place.index(mask))
            parts.append(g_ref[at : at + 64, :])
    rows = jnp.concatenate(parts, axis=0)
    out[:, :1024] = dot(rows[:, :512], w_ref[:, q * 1024 : q * 1024 + 1024]).astype(bf16)
    if out.shape[1] > 1024:
        out[:, 1024:] = rows[:, 512:]


def gate_kernel(masks, name, y_ref, bc_ref, grow_ref, before_ref, states_hbm, z_hbm, sin_ref, gain_ref, w_ref, *rest):
    count = len(masks)
    far = name == "gate_far"
    if far:
        outs, (st, g, w, zs, ss, b0, b1, b2, b3, sems) = rest[:5], rest[5:]
    else:
        g_before, outs = rest[0], rest[1:6]
        st, g, w, zs, ss, b0, b1, b2, b3, sems = rest[6:]
    i = pl.program_id(0)
    here = lax.axis_index("head")
    bufs = (b0, b1, b2, b3)

    def mask_of(k):
        mask = jnp.int32(masks[0])
        for n in range(1, count):
            mask = jnp.where(k == n, masks[n], mask)
        return mask

    def out_copy(n):
        return pltpu.make_async_copy(g if n == 4 else bufs[n], outs[n], sems.at[n])

    def w_copy(q):
        cols = slice(1024 * q, 1024 * q + 1024)
        return pltpu.make_async_copy(w_ref.at[:, cols], w.at[:, cols], sems.at[5 + q])

    def in_copies(k):
        owner = jnp.bitwise_xor(here, mask_of(k))
        rows = pl.ds(pl.multiple_of(owner * 64, 64), 64)
        chunk = pl.ds(pl.multiple_of(owner // 2 * Q, Q), Q)
        return (
            pltpu.make_async_copy(
                z_hbm.at[rows, :], zs.at[pl.ds(pl.multiple_of(k * 64, 64), 64), :], sems.at[9 + k]
            ),
            pltpu.make_async_copy(
                states_hbm.at[chunk, :],
                ss.at[pl.ds(pl.multiple_of(k * Q, Q), Q), :],
                sems.at[18 + k],
            ),
        )

    @pl.when(i == 0)
    def _():
        for k in range(count):
            for copy in in_copies(k):
                copy.start()
        for q in range(4):
            w_copy(q).start()
        for j in range(16):
            group, p = j // 4, j % 4
            st[32 * group : 32 * group + 32, 128 * p : 128 * p + 128] = sin_ref[j].astype(f32)
        if not far:
            for n, mask in enumerate(FIRST):
                g[64 * mask : 64 * mask + 64, :] = g_before[64 * n : 64 * n + 64, :]

    @pl.when(i < count)
    def _():
        for copy in in_copies(i):
            copy.wait()
        mask = mask_of(i)
        owner = jnp.bitwise_xor(here, mask)
        rows = pl.ds(pl.multiple_of(owner * 64, 64), 64)
        lanes = pl.ds(pl.multiple_of(owner // 2 * Q, Q), Q)
        mine = pl.ds(pl.multiple_of(i * 64, 64), 64)
        target = mine if far else pl.ds(pl.multiple_of(mask * 64, 64), 64)
        chunk = pl.ds(pl.multiple_of(i * Q, Q), Q)
        before = jnp.exp(before_ref[:, lanes])
        low1 = lax.broadcasted_iota(jnp.int32, (1, 128), 1) < 64
        grow = dot(grow_ref[rows, :], spread())
        c = bc_ref[rows, 128:]
        squares = jnp.zeros((64, 128), f32)
        for p in range(4):
            cols = slice(128 * p, 128 * p + 128)
            entering = ss[chunk, cols].astype(f32) + st[:, cols] * pair_row(low1, before, 2 * p)
            ssd = y_ref[rows, cols] + grow[:, cols] * dot(c, entering.astype(bf16))
            v = ssd * silu(zs[mine, cols].astype(f32))
            squares = squares + v * v
            g[target, cols] = (v * gain_ref[:, cols]).astype(bf16)
        g[target, 512:] = dot(squares.astype(bf16), jnp.ones((128, 128), bf16)).astype(bf16)

    for q, (ax, m, _) in enumerate(SETS):

        @pl.when(i == count + q)
        def _(q=q, ax=ax, m=m):
            w_copy(q).wait()
            if far:
                projected(g, w, q, bufs[q], ax, (2,), FIRST)
            else:
                projected(g, w, q, bufs[q], ax, (m,))
            out_copy(q).start()

    @pl.when(i == count)
    def _():
        out_copy(4).start()

    @pl.when(i == count + 3)
    def _():
        for n in range(5):
            out_copy(n).wait()


def gate(name, masks, y, bc, grow, before, states, z_gate, incoming, gain, w_out, *g_before):
    anywhere = pl.BlockSpec(memory_space=pl.ANY)
    near = pl.BlockSpec(memory_space=pltpu.VMEM)
    count = len(masks)
    g_rows = 1024 if g_before else count * 64
    return pl.pallas_call(
        functools.partial(gate_kernel, masks, name),
        grid=(count + 4,),
        in_specs=[near, near, near, near, anywhere, anywhere, near, near, anywhere]
        + [near] * len(g_before),
        out_specs=[anywhere] * 5,
        out_shape=[jax.ShapeDtypeStruct((256, n), bf16) for n in WIDTHS]
        + [jax.ShapeDtypeStruct((g_rows, 640), bf16)],
        scratch_shapes=[
            pltpu.VMEM((128, 512), f32),
            pltpu.VMEM((g_rows, 640), bf16),
            pltpu.VMEM((512, 4096), bf16),
            pltpu.VMEM((count * 64, 512), bf16),
            pltpu.VMEM((count * Q, 512), bf16),
        ]
        + [pltpu.VMEM((256, n), bf16) for n in WIDTHS]
        + [pltpu.SemaphoreType.DMA((27,))],
        compiler_params=PARAMS,
    )(
        y, bc, grow, before, in_hbm(states), in_hbm(z_gate), incoming, gain, in_hbm(w_out),
        *g_before,
    )


def keep_kernel(g_ref, w_ref, *rest):
    outs, (b0, b1, b2, b3, sems) = rest[:8], rest[8:]
    bufs = (b0, b1, b2, b3)
    i = pl.program_id(0)

    def out_copy(n):
        q, part = n % 4, n // 4
        return pltpu.make_async_copy(
            bufs[q].at[part * 256 : part * 256 + 256], outs[n], sems.at[n]
        )

    for q, (ax, m, _) in enumerate(SETS):

        @pl.when(i == q)
        def _(q=q, ax=ax, m=m):
            projected(g_ref, w_ref, q, bufs[q], ax, (m ^ 2, 0))
            out_copy(q).start()
            out_copy(4 + q).start()

    @pl.when(i == 3)
    def _():
        for n in range(8):
            out_copy(n).wait()


def keep(g, w_out):
    return pl.pallas_call(
        keep_kernel,
        grid=(4,),
        in_specs=[
            pl.BlockSpec(memory_space=pltpu.VMEM),
            pl.BlockSpec(memory_space=pltpu.VMEM),
        ],
        out_specs=[pl.BlockSpec(memory_space=pl.ANY)] * 8,
        out_shape=[jax.ShapeDtypeStruct((256, n), bf16) for n in WIDTHS * 2],
        scratch_shapes=[pltpu.VMEM((512, n), bf16) for n in WIDTHS]
        + [pltpu.SemaphoreType.DMA((8,))],
        name="keep",
        compiler_params=PARAMS,
    )(g, pltpu.with_memory_space_constraint(w_out, pltpu.VMEM))


def swap(values, axis, mask):
    mask = mask * 4 if axis == 0 else mask
    return lax.ppermute(values, "head", [(h, h ^ mask) for h in range(16)])


def added(*values):
    total = values[0].astype(f32)
    for v in values[1:]:
        total = total + v.astype(f32)
    return total


def summed_to_owners(gated, w_out):
    *sends, g_first = gate("gate_far", FIRST, *gated)
    far = []
    for q, (ax, m, _) in enumerate(SETS):
        far.append(swap(sends[q], ax, m))
    *sends, g = gate("gate_near", REST, *gated, g_first)
    near = []
    for q, (ax, m, _) in enumerate(SETS):
        near.append(swap(sends[q], ax, m))
    kept = keep(g, w_out)
    passed, own = kept[:4], kept[4:]
    second = [
        swap(added(a, b).astype(bf16), ax, m ^ 2) for a, b, (ax, m, q) in zip(passed, far, SETS)
    ]
    later = []
    for (ax, m, q), a, b, c in zip(SETS, own, near, second):
        total = added(a, b, c).reshape(4, 64, -1)
        away = jnp.stack([total[m], total[2]]).astype(bf16)
        later.append((total[0], total[m ^ 2], swap(away, 1 - ax, m)))
    last = []
    for (ax, m, q), (first, second, got) in zip(SETS, later):
        last.append(
            (
                added(first, got[0]),
                swap(added(second, got[1]).astype(bf16), 1 - ax, m ^ 2),
            )
        )
    parts = [added(a, b) for a, b in last]
    scale = lax.rsqrt(parts[0][:, 1024:1025] / INNER + norm_eps)
    return jnp.concatenate([v[:, :1024] * scale for v in parts], axis=1).astype(bf16)


def layer(x_in, z_gate, b_in, c_in, dt_raw, a_log, d_skip, conv_x, conv_bc, norm_gain, w_out):
    rim = lax.ppermute(
        edge_rows(x_in, b_in, c_in), "seq", [(i, i + 1) for i in range(15)]
    )
    run, step, late, grow = decays(dt_raw, a_log)
    xc, bc, before, states, msg = block_states(
        x_in, b_in, c_in, rim, run, late, conv_x, conv_bc
    )
    pieces = prefix(lax.all_to_all(msg, "seq", 0, 0))
    incoming = lax.all_to_all(pieces, "seq", 0, 0)
    y = inside(xc, bc, run, step, d_skip)
    gated = (y, bc, grow, before, states, z_gate, incoming, norm_gain[None, :], w_out)
    return summed_to_owners(gated, w_out)


def solution(mesh):
    in_specs = (
        P("seq", "head"),
        P("seq", "head"),
        P("seq", None),
        P("seq", None),
        P("seq", "head"),
        P("head"),
        P("head"),
        P(None, "head"),
        P(),
        P("head"),
        P("head", None),
    )
    out_specs = P(("seq", "head"), None)
    return jax.shard_map(layer, mesh=mesh, in_specs=in_specs, out_specs=out_specs, check_vma=False)
```

```python
import functools

import jax
import jax.numpy as jnp
from jax import lax
from jax.experimental import pallas as pl
from jax.experimental.pallas import tpu as pltpu
from jax.sharding import PartitionSpec as P


INNER = 8192
norm_eps = 1e-05
Q = 128
PARAMS = pltpu.CompilerParams(vmem_limit_bytes=24 * 2**20)
bf16 = jnp.bfloat16
f32 = jnp.float32


def in_hbm(v):
    return pltpu.with_memory_space_constraint(v, pltpu.HBM)


def silu(v):
    half = 0.5 * v
    return half + half * jnp.tanh(half)


def dot(a, b):
    return jnp.dot(a, b, preferred_element_type=f32)


def dot_t(a, b):
    return lax.dot_general(a, b, (((1,), (1,)), ((), ())), preferred_element_type=f32)


def head_column(ref, shape):
    rows = lax.broadcasted_iota(jnp.int32, shape, 0)
    out = jnp.full(shape, ref[0], f32)
    for h in range(1, 8):
        out = jnp.where(rows == h, ref[h], out)
    return out


def edge_kernel(x_ref, b_ref, c_ref, o_ref):
    o_ref[:, :512] = x_ref[...]
    o_ref[:, 512:640] = b_ref[...]
    o_ref[:, 640:] = c_ref[...]


def edge_rows(x_in, b_in, c_in):
    last = lambda n: pl.BlockSpec((16, n), lambda i: (63, 0))
    return pl.pallas_call(
        edge_kernel,
        grid=(1,),
        in_specs=[last(512), last(128), last(128)],
        out_specs=pl.BlockSpec((16, 768), lambda i: (0, 0)),
        out_shape=jax.ShapeDtypeStruct((16, 768), bf16),
        name="edge",
        compiler_params=PARAMS,
    )(in_hbm(x_in), in_hbm(b_in), in_hbm(c_in))


def pair_row(low, values, h):
    return jnp.where(low, values[h : h + 1, :], values[h + 1 : h + 2, :])


def decay_kernel(a_ref, dt_ref, run_ref, step_ref, late_ref, grow_ref):
    rate = -jnp.exp(head_column(a_ref, (8, Q)))
    lane8 = lax.broadcasted_iota(jnp.int32, (8, Q), 1)

    def halves(v):
        high = v.astype(bf16).astype(f32)
        return jnp.transpose(jnp.concatenate([high, v - high], axis=0)).astype(bf16)

    for i in range(1024 // Q):
        lanes = slice(i * Q, i * Q + Q)
        raw = dt_ref[:, lanes]
        dt = jnp.maximum(raw, 0.0) + jnp.log1p(jnp.exp(-jnp.abs(raw)))
        run = rate * dt
        shift = 1
        while shift < Q:
            run = run + jnp.where(lane8 >= shift, pltpu.roll(run, shift, 1), 0.0)
            shift *= 2
        fin = jnp.broadcast_to(run[:, Q - 1 : Q], (8, Q))
        run_ref[:, lanes] = run
        step_ref[:, lanes] = dt
        late_ref[lanes, :] = halves(jnp.exp(jnp.minimum(fin - run, 0.0)) * dt)
        grow_ref[lanes, :] = halves(jnp.exp(run))


def decays(dt_raw, a_log):
    full = lambda *s: pl.BlockSpec(s, lambda i: (0,) * len(s))
    return pl.pallas_call(
        decay_kernel,
        grid=(1,),
        in_specs=[pl.BlockSpec(memory_space=pltpu.SMEM), full(8, 1024)],
        out_specs=[full(8, 1024)] * 2 + [full(1024, 16)] * 2,
        out_shape=[jax.ShapeDtypeStruct((8, 1024), f32)] * 2
        + [jax.ShapeDtypeStruct((1024, 16), bf16)] * 2,
        name="decays",
        compiler_params=PARAMS,
    )(a_log, dt_raw.T)


def spread():
    lane = lax.broadcasted_iota(jnp.int32, (16, 512), 1)
    row = lax.broadcasted_iota(jnp.int32, (16, 512), 0)
    first = jnp.where(row >= 8, row - 8, row) * 64
    return jnp.where((lane >= first) & (lane < first + 64), 1.0, 0.0).astype(bf16)


def state_kernel(
    x_ref, b_ref, c_ref, rim_ref, run_ref, late_ref, wx_ref, wbc_ref,
    xc_hbm, bc_ref, before_ref, states_hbm, msg_ref,
    xs, bs, st, tot, xc_ref, states_ref, sems,
):
    i = pl.program_id(0)
    here = pl.ds(pl.multiple_of(i * Q, Q), Q)

    def out_copies(k):
        part = pl.ds(pl.multiple_of(k * Q, Q), Q)
        return (
            pltpu.make_async_copy(xc_ref.at[part, :], xc_hbm.at[part, :], sems.at[k]),
            pltpu.make_async_copy(states_ref.at[part, :], states_hbm.at[part, :], sems.at[8 + k]),
        )

    @pl.when(i == 0)
    def _():
        xs[0:8, :] = rim_ref[8:16, :512].astype(f32)
        bs[0:8, :] = rim_ref[8:16, 512:].astype(f32)
        st[...] = jnp.zeros_like(st)
        tot[...] = jnp.zeros_like(tot)

    @pl.when(i > 0)
    def _():
        xs[0:8, :] = xs[Q : Q + 8, :]
        bs[0:8, :] = bs[Q : Q + 8, :]

    xs[8 : Q + 8, :] = x_ref[...].astype(f32)
    bs[8 : Q + 8, :128] = b_ref[...].astype(f32)
    bs[8 : Q + 8, 128:] = c_ref[...].astype(f32)

    def conv(buf, w_ref, cols):
        whole = buf[:, cols]
        half = 0.5 * w_ref[:, cols]
        total = half[3:4] * whole[8:]
        for k in range(3):
            total = total + half[k : k + 1] * pltpu.roll(whole, 3 - k, 0)[8:]
        return total + total * jnp.tanh(total)

    fin = jnp.broadcast_to(run_ref[:, Q - 1 : Q], (8, 128))
    b = conv(bs, wbc_ref, slice(0, 128))
    bc_ref[:, :128] = b.astype(bf16)
    bc_ref[:, 128:] = conv(bs, wbc_ref, slice(128, 256)).astype(bf16)
    b_t = jnp.transpose(b).astype(bf16)
    low1 = lax.broadcasted_iota(jnp.int32, (1, 128), 1) < 64
    late = dot(late_ref[...], spread())
    states_ref[here, :] = st[...].astype(bf16)
    before_ref[...] = tot[...]
    for p in range(4):
        cols = slice(128 * p, 128 * p + 128)
        xp = conv(xs, wx_ref, cols)
        xc_ref[here, cols] = xp.astype(bf16)
        end = jnp.exp(pair_row(low1, fin, 2 * p))
        st[:, cols] = st[:, cols] * end + dot(b_t, (xp * late[:, cols]).astype(bf16))
    tot[...] = tot[...] + fin
    for copy in out_copies(i):
        copy.start()

    @pl.when(i == pl.num_programs(0) - 1)
    def _():
        total = tot[...]
        row8 = lax.broadcasted_iota(jnp.int32, (8, 128), 0)
        for p in range(4):
            decay = jnp.broadcast_to(pair_row(low1, total, 2 * p), (8, 128))
            high = decay.astype(bf16).astype(f32)
            tile = jnp.where(row8 == 0, high, decay - high).astype(bf16)
            for group in range(4):
                j = 4 * group + p
                msg_ref[j, 0:32, :] = st[
                    32 * group : 32 * group + 32, 128 * p : 128 * p + 128
                ].astype(bf16)
                msg_ref[j, 32:40, :] = tile
        for k in range(8):
            for copy in out_copies(k):
                copy.wait()


def block_states(x_in, b_in, c_in, rim, run, late, conv_x, conv_bc):
    rows = lambda n: pl.BlockSpec((Q, n), lambda i: (i, 0))
    full = lambda *s: pl.BlockSpec(s, lambda i: (0,) * len(s))
    lanes = pl.BlockSpec((8, Q), lambda i: (0, i))
    anywhere = pl.BlockSpec(memory_space=pl.ANY)
    return pl.pallas_call(
        state_kernel,
        grid=(1024 // Q,),
        in_specs=[
            rows(512), rows(128), rows(128), full(16, 768), lanes, rows(16),
            full(4, 512), full(4, 256),
        ],
        out_specs=[anywhere, rows(256), lanes, anywhere, full(16, 40, 128)],
        out_shape=[
            pltpu.HBM((1024, 512), bf16),
            jax.ShapeDtypeStruct((1024, 256), bf16),
            jax.ShapeDtypeStruct((8, 1024), f32),
            pltpu.HBM((1024, 512), bf16),
            jax.ShapeDtypeStruct((16, 40, 128), bf16),
        ],
        scratch_shapes=[
            pltpu.VMEM((Q + 8, 512), f32),
            pltpu.VMEM((Q + 8, 256), f32),
            pltpu.VMEM((128, 512), f32),
            pltpu.VMEM((8, Q), f32),
            pltpu.VMEM((1024, 512), bf16),
            pltpu.VMEM((1024, 512), bf16),
            pltpu.SemaphoreType.DMA((16,)),
        ],
        name="states",
        compiler_params=PARAMS,
    )(x_in, b_in, c_in, rim, run, late, conv_x, conv_bc)


def inside_kernel(skip_ref, xc_ref, bc_ref, run_ref, step_ref, y_ref):
    b = bc_ref[:, :128]
    c = bc_ref[:, 128:]
    run = run_ref[...]
    dt = step_ref[...]
    run_t = jnp.transpose(run)
    row = lax.broadcasted_iota(jnp.int32, (Q, Q), 0)
    col = lax.broadcasted_iota(jnp.int32, (Q, Q), 1)
    scores = jnp.where(row >= col, dot_t(c, b), 0.0)
    low = col < 64
    for p in range(4):
        h = 2 * p
        cols = slice(128 * p, 128 * p + 128)
        xf = xc_ref[:, cols].astype(f32)
        xb = jnp.concatenate(
            [jnp.where(low, xf, 0.0).astype(bf16), jnp.where(low, 0.0, xf).astype(bf16)], axis=0
        )
        mix = []
        for k in (h, h + 1):
            fade = jnp.exp(jnp.minimum(run_t[:, k : k + 1] - run[k : k + 1, :], 0.0))
            mix.append((fade * scores * dt[k : k + 1, :]).astype(bf16))
        skip = jnp.where(low[:1], skip_ref[h], skip_ref[h + 1])
        y_ref[:, cols] = dot(jnp.concatenate(mix, axis=1), xb) + skip * xf


def inside(xc, bc, run, step, d_skip):
    rows = lambda n: pl.BlockSpec((Q, n), lambda i: (i, 0))
    lanes = pl.BlockSpec((8, Q), lambda i: (0, i))
    return pl.pallas_call(
        inside_kernel,
        grid=(1024 // Q,),
        in_specs=[
            pl.BlockSpec(memory_space=pltpu.SMEM), rows(512), rows(256), lanes, lanes,
        ],
        out_specs=rows(512),
        out_shape=jax.ShapeDtypeStruct((1024, 512), f32),
        name="inside",
        compiler_params=PARAMS,
    )(d_skip, in_hbm(xc), bc, run, step)


def prefix_kernel(in_ref, out_ref):
    acc = jnp.zeros((32, 128), f32)
    for j in range(16):
        out_ref[j] = acc.astype(bf16)
        if j < 15:
            t = in_ref[j, 32:40, :].astype(f32)
            decay = jnp.exp(t[0:1] + t[1:2])
            acc = acc * decay + in_ref[j, 0:32, :].astype(f32)


def prefix(msg):
    return pl.pallas_call(
        prefix_kernel, out_shape=jax.ShapeDtypeStruct((16, 32, 128), bf16), name="prefix",
        compiler_params=PARAMS
    )(msg)


SETS = ((0, 1, 0), (0, 3, 1), (1, 1, 2), (1, 3, 3))
WIDTHS = (1152, 1024, 1024, 1024)


FIRST = (8, 9, 10, 11, 2, 6, 14)
REST = (0, 1, 3, 4, 5, 7, 12, 13, 15)


def projected(g_ref, w_ref, q, out, axis, picks, place=None):
    parts = []
    for pick in picks:
        for k in range(4):
            mask = pick * 4 + k if axis == 0 else k * 4 + pick
            at = 64 * (mask if place is None else place.index(mask))
            parts.append(g_ref[at : at + 64, :])
    rows = jnp.concatenate(parts, axis=0)
    out[:, :1024] = dot(rows[:, :512], w_ref[:, q * 1024 : q * 1024 + 1024]).astype(bf16)
    if out.shape[1] > 1024:
        out[:, 1024:] = rows[:, 512:]


def gate_kernel(masks, name, y_ref, bc_ref, grow_ref, before_ref, states_hbm, z_hbm, sin_ref, gain_ref, w_ref, *rest):
    count = len(masks)
    far = name == "gate_far"
    if far:
        outs, (st, g, w, zs, ss, b0, b1, b2, b3, sems) = rest[:5], rest[5:]
    else:
        g_before, outs = rest[0], rest[1:6]
        st, g, w, zs, ss, b0, b1, b2, b3, sems = rest[6:]
    i = pl.program_id(0)
    here = lax.axis_index("head")
    bufs = (b0, b1, b2, b3)

    def mask_of(k):
        mask = jnp.int32(masks[0])
        for n in range(1, count):
            mask = jnp.where(k == n, masks[n], mask)
        return mask

    def out_copy(n):
        return pltpu.make_async_copy(g if n == 4 else bufs[n], outs[n], sems.at[n])

    def w_copy(q):
        cols = slice(1024 * q, 1024 * q + 1024)
        return pltpu.make_async_copy(w_ref.at[:, cols], w.at[:, cols], sems.at[5 + q])

    def in_copies(k):
        owner = jnp.bitwise_xor(here, mask_of(k))
        rows = pl.ds(pl.multiple_of(owner * 64, 64), 64)
        chunk = pl.ds(pl.multiple_of(owner // 2 * Q, Q), Q)
        return (
            pltpu.make_async_copy(
                z_hbm.at[rows, :], zs.at[pl.ds(pl.multiple_of(k * 64, 64), 64), :], sems.at[9 + k]
            ),
            pltpu.make_async_copy(
                states_hbm.at[chunk, :],
                ss.at[pl.ds(pl.multiple_of(k * Q, Q), Q), :],
                sems.at[18 + k],
            ),
        )

    @pl.when(i == 0)
    def _():
        for k in range(count):
            for copy in in_copies(k):
                copy.start()
        for q in range(4):
            w_copy(q).start()
        for j in range(16):
            group, p = j // 4, j % 4
            st[32 * group : 32 * group + 32, 128 * p : 128 * p + 128] = sin_ref[j].astype(f32)
        if not far:
            for n, mask in enumerate(FIRST):
                g[64 * mask : 64 * mask + 64, :] = g_before[64 * n : 64 * n + 64, :]

    @pl.when(i < count)
    def _():
        for copy in in_copies(i):
            copy.wait()
        mask = mask_of(i)
        owner = jnp.bitwise_xor(here, mask)
        rows = pl.ds(pl.multiple_of(owner * 64, 64), 64)
        lanes = pl.ds(pl.multiple_of(owner // 2 * Q, Q), Q)
        mine = pl.ds(pl.multiple_of(i * 64, 64), 64)
        target = mine if far else pl.ds(pl.multiple_of(mask * 64, 64), 64)
        chunk = pl.ds(pl.multiple_of(i * Q, Q), Q)
        before = jnp.exp(before_ref[:, lanes])
        low1 = lax.broadcasted_iota(jnp.int32, (1, 128), 1) < 64
        grow = dot(grow_ref[rows, :], spread())
        c = bc_ref[rows, 128:]
        squares = jnp.zeros((64, 128), f32)
        for p in range(4):
            cols = slice(128 * p, 128 * p + 128)
            entering = ss[chunk, cols].astype(f32) + st[:, cols] * pair_row(low1, before, 2 * p)
            ssd = y_ref[rows, cols] + grow[:, cols] * dot(c, entering.astype(bf16))
            v = ssd * silu(zs[mine, cols].astype(f32))
            squares = squares + v * v
            g[target, cols] = (v * gain_ref[:, cols]).astype(bf16)
        g[target, 512:] = dot(squares.astype(bf16), jnp.ones((128, 128), bf16)).astype(bf16)

    for q, (ax, m, _) in enumerate(SETS):

        @pl.when(i == count + q)
        def _(q=q, ax=ax, m=m):
            w_copy(q).wait()
            if far:
                projected(g, w, q, bufs[q], ax, (2,), FIRST)
            else:
                projected(g, w, q, bufs[q], ax, (m,))
            out_copy(q).start()

    @pl.when(i == count)
    def _():
        out_copy(4).start()

    @pl.when(i == count + 3)
    def _():
        for n in range(5):
            out_copy(n).wait()


def gate(name, masks, y, bc, grow, before, states, z_gate, incoming, gain, w_out, *g_before):
    anywhere = pl.BlockSpec(memory_space=pl.ANY)
    near = pl.BlockSpec(memory_space=pltpu.VMEM)
    count = len(masks)
    g_rows = 1024 if g_before else count * 64
    return pl.pallas_call(
        functools.partial(gate_kernel, masks, name),
        grid=(count + 4,),
        in_specs=[near, near, near, near, anywhere, anywhere, near, near, anywhere]
        + [near] * len(g_before),
        out_specs=[anywhere] * 5,
        out_shape=[jax.ShapeDtypeStruct((256, n), bf16) for n in WIDTHS]
        + [jax.ShapeDtypeStruct((g_rows, 640), bf16)],
        scratch_shapes=[
            pltpu.VMEM((128, 512), f32),
            pltpu.VMEM((g_rows, 640), bf16),
            pltpu.VMEM((512, 4096), bf16),
            pltpu.VMEM((count * 64, 512), bf16),
            pltpu.VMEM((count * Q, 512), bf16),
        ]
        + [pltpu.VMEM((256, n), bf16) for n in WIDTHS]
        + [pltpu.SemaphoreType.DMA((27,))],
        compiler_params=PARAMS,
    )(
        y, bc, grow, before, in_hbm(states), in_hbm(z_gate), incoming, gain, in_hbm(w_out),
        *g_before,
    )


def keep_kernel(g_ref, w_ref, *rest):
    outs, (b0, b1, b2, b3, sems) = rest[:8], rest[8:]
    bufs = (b0, b1, b2, b3)
    i = pl.program_id(0)

    def out_copy(n):
        q, part = n % 4, n // 4
        return pltpu.make_async_copy(
            bufs[q].at[part * 256 : part * 256 + 256], outs[n], sems.at[n]
        )

    for q, (ax, m, _) in enumerate(SETS):

        @pl.when(i == q)
        def _(q=q, ax=ax, m=m):
            projected(g_ref, w_ref, q, bufs[q], ax, (m ^ 2, 0))
            out_copy(q).start()
            out_copy(4 + q).start()

    @pl.when(i == 3)
    def _():
        for n in range(8):
            out_copy(n).wait()


def keep(g, w_out):
    return pl.pallas_call(
        keep_kernel,
        grid=(4,),
        in_specs=[
            pl.BlockSpec(memory_space=pltpu.VMEM),
            pl.BlockSpec(memory_space=pltpu.VMEM),
        ],
        out_specs=[pl.BlockSpec(memory_space=pl.ANY)] * 8,
        out_shape=[jax.ShapeDtypeStruct((256, n), bf16) for n in WIDTHS * 2],
        scratch_shapes=[pltpu.VMEM((512, n), bf16) for n in WIDTHS]
        + [pltpu.SemaphoreType.DMA((8,))],
        name="keep",
        compiler_params=PARAMS,
    )(g, pltpu.with_memory_space_constraint(w_out, pltpu.VMEM))


def swap(values, axis, mask):
    mask = mask * 4 if axis == 0 else mask
    return lax.ppermute(values, "head", [(h, h ^ mask) for h in range(16)])


def added(*values):
    total = values[0].astype(f32)
    for v in values[1:]:
        total = total + v.astype(f32)
    return total


def summed_to_owners(gated, w_out):
    *sends, g_first = gate("gate_far", FIRST, *gated)
    far = []
    for q, (ax, m, _) in enumerate(SETS):
        far.append(swap(sends[q], ax, m))
    *sends, g = gate("gate_near", REST, *gated, g_first)
    near = []
    for q, (ax, m, _) in enumerate(SETS):
        near.append(swap(sends[q], ax, m))
    kept = keep(g, w_out)
    passed, own = kept[:4], kept[4:]
    second = [
        swap(added(a, b).astype(bf16), ax, m ^ 2) for a, b, (ax, m, q) in zip(passed, far, SETS)
    ]
    total = [added(a, b, c).reshape(4, 64, -1) for a, b, c in zip(own, near, second)]

    def swaps(values, masks):
        out = []
        for q, (ax, m, _) in enumerate(SETS):
            out.append(swap(values[q].astype(bf16), 1 - ax, masks[q]))
        return out

    near_to = [m for _, m, _ in SETS]
    pass_to = [m ^ 2 for m in near_to]
    later_far = swaps([t[2] for t in total], near_to)
    later_near = swaps([t[m] for t, m in zip(total, near_to)], near_to)
    last = swaps([added(t[m], a) for t, m, a in zip(total, pass_to, later_far)], pass_to)
    parts = [added(t[0], a, b) for t, a, b in zip(total, later_near, last)]
    scale = lax.rsqrt(parts[0][:, 1024:1025] / INNER + norm_eps)
    return jnp.concatenate([v[:, :1024] * scale for v in parts], axis=1).astype(bf16)


def layer(x_in, z_gate, b_in, c_in, dt_raw, a_log, d_skip, conv_x, conv_bc, norm_gain, w_out):
    rim = lax.ppermute(
        edge_rows(x_in, b_in, c_in), "seq", [(i, i + 1) for i in range(15)]
    )
    run, step, late, grow = decays(dt_raw, a_log)
    xc, bc, before, states, msg = block_states(
        x_in, b_in, c_in, rim, run, late, conv_x, conv_bc
    )
    pieces = prefix(lax.all_to_all(msg, "seq", 0, 0))
    incoming = lax.all_to_all(pieces, "seq", 0, 0)
    y = inside(xc, bc, run, step, d_skip)
    gated = (y, bc, grow, before, states, z_gate, incoming, norm_gain[None, :], w_out)
    return summed_to_owners(gated, w_out)


def solution(mesh):
    in_specs = (
        P("seq", "head"),
        P("seq", "head"),
        P("seq", None),
        P("seq", None),
        P("seq", "head"),
        P("head"),
        P("head"),
        P(None, "head"),
        P(),
        P("head"),
        P("head", None),
    )
    out_specs = P(("seq", "head"), None)
    return jax.shard_map(layer, mesh=mesh, in_specs=in_specs, out_specs=out_specs, check_vma=False)
```
